1024 devices in a mesh: dom: 32 (over y, x, core), head: 32 (over z).
Axes of the slice: x: 4, y: 4, z: 32, core: 2. Of those that a mesh axis runs over, the one named last changes fastest.
Arguments:
- queries: bfloat16 [18432, 2048], P(('dom', 'head')), may hold values from -8 to 8
- keys_in: bfloat16 [18432, 2048], P(('dom', 'head')), may hold values from -8 to 8
- values_in: bfloat16 [18432, 2048], P(('dom', 'head')), may hold values from -6 to 6
- grad_out: bfloat16 [18432, 2048], P(('dom', 'head')), may hold values from -6 to 6
- pos_bias: float32 [32, 64, 576], P('head'), may hold values from -4 to 4
- neighbours: int32 [288, 9], P('dom'), may hold values from 0 to 32, as said below
- send_block: int32 [32, 8, 3], P('dom'), may hold values from 0 to 8, as said below
- orient: int32 [32, 8], P('dom'), may hold values from 0 to 7
Outputs:
- grad_q: bfloat16 [18432, 2048], P(('dom', 'head'))
- grad_k: bfloat16 [18432, 2048], P(('dom', 'head'))
- grad_v: bfloat16 [18432, 2048], P(('dom', 'head'))
The draws below stay inside these ranges and needn't reach their ends.
Inputs may be any that keep to these rules, and one draw needn't show every extreme that they name: `neighbours`: entry [d * 9 + b, j] names the j-th key block of query block b of domain d: e below 9 is the domain's own block e, and 9 + k * 3 + c is slot c of what domain d borrows from direction k. The 9 entries of a query block are distinct and name only live slots of send_block. `send_block`: entry [p, k, c] is the block that domain p lends in slot c to the domain d with nb(d, k) = p. The live slots of one entry [p, k] name distinct blocks; there are 3 of them for the four edge directions and one for the four corner directions, none where no such d exists; slots that are not live hold 0 and no neighbours entry names them.
All inputs are finite; a program needn't handle non-finite values.
Results may differ from the reference program's by a relative error of at most 0.025.
Values may be sent and summed in bfloat16 or wider, within the bound.
A program may use at most 32 MiB of HBM per device.

```python
import jax
import jax.numpy as jnp
import numpy as np
from jax import lax

HEADS = 32
HD = 64
D = 2048
PATCH = 8
BT = 64
TILE = 3
GRID_ROWS = 4
DIRS = 8
WIN = 9
WINK = 576
QB_DOM = 9
DOMAINS = 32
TOKENS = 18432
CAP = 3


def grid_layout(key):
    grid_cols = DOMAINS // GRID_ROWS
    domain_ids = jnp.arange(DOMAINS, dtype=jnp.int32)
    cell_row = domain_ids // grid_cols
    cell_col = domain_ids % grid_cols
    block_ids = jnp.arange(QB_DOM, dtype=jnp.int32)
    glob_row = cell_row[:, None] * TILE + block_ids[None, :] // TILE
    glob_col = cell_col[:, None] * TILE + block_ids[None, :] % TILE
    centre_row = jnp.clip(glob_row, 1, GRID_ROWS * TILE - 2)
    centre_col = jnp.clip(glob_col, 1, grid_cols * TILE - 2)
    step_row = jnp.array([-1, -1, -1, 0, 0, 0, 1, 1, 1], jnp.int32)
    step_col = jnp.array([-1, 0, 1, -1, 0, 1, -1, 0, 1], jnp.int32)
    key_row = centre_row[:, :, None] + step_row
    key_col = centre_col[:, :, None] + step_col
    tile_row = key_row // TILE
    tile_col = key_col // TILE
    owner_dom = tile_row * grid_cols + tile_col
    local_row = key_row % TILE
    local_col = key_col % TILE
    shift_row = tile_row - cell_row[:, None, None]
    shift_col = tile_col - cell_col[:, None, None]
    slot_pos = jnp.where(shift_row == 0, local_row, jnp.where(shift_col == 0, local_col, 0))
    flat_dir = (shift_row + 1) * 3 + (shift_col + 1)
    direction = jnp.clip(jnp.where(flat_dir > 4, flat_dir - 1, flat_dir), 0, DIRS - 1)
    slot_keys = jax.random.split(jax.random.fold_in(key, 101), DOMAINS * DIRS)
    slot_perm = jax.vmap(lambda one_key: jax.random.permutation(one_key, CAP))(slot_keys)
    slot_perm = slot_perm.reshape(DOMAINS, DIRS, CAP).astype(jnp.int32)
    dom_index = jnp.broadcast_to(domain_ids[:, None, None], direction.shape)
    slot_num = slot_perm[dom_index, direction, slot_pos]
    is_mine = owner_dom == domain_ids[:, None, None]
    near = jnp.where(is_mine, local_row * TILE + local_col, QB_DOM + direction * CAP + slot_num)
    near = near.reshape(DOMAINS * QB_DOM, WIN).astype(jnp.int32)
    order_keys = jax.random.split(jax.random.fold_in(key, 102), DOMAINS * QB_DOM)
    orders = jax.vmap(lambda one_key: jax.random.permutation(one_key, WIN))(order_keys).astype(jnp.int32)
    near = jnp.take_along_axis(near, orders, axis=1).astype(jnp.int32)
    off_row = jnp.array([-1, -1, -1, 0, 0, 1, 1, 1], jnp.int32)
    off_col = jnp.array([-1, 0, 1, -1, 1, -1, 0, 1], jnp.int32)
    recv_row = cell_row[:, None] - off_row[None, :]
    recv_col = cell_col[:, None] - off_col[None, :]
    valid = (recv_row >= 0) & (recv_row < GRID_ROWS) & (recv_col >= 0) & (recv_col < grid_cols)
    recv_dom = jnp.clip(recv_row, 0, GRID_ROWS - 1) * grid_cols + jnp.clip(recv_col, 0, grid_cols - 1)
    corner = (off_row != 0) & (off_col != 0)
    send_count = jnp.where(valid, jnp.where(corner[None, :], 1, TILE), 0)
    position = jnp.arange(CAP, dtype=jnp.int32)[None, None, :]
    row_dir = off_row[None, :, None]
    col_dir = off_col[None, :, None]
    pick_row = jnp.where(row_dir == 1, 0, jnp.where(row_dir == -1, TILE - 1, position))
    pick_col = jnp.where(col_dir == 1, 0, jnp.where(col_dir == -1, TILE - 1, position))
    values = jnp.where(position < send_count[:, :, None], pick_row * TILE + pick_col, 0).astype(jnp.int32)
    shape3 = (DOMAINS, DIRS, CAP)
    dir_index = jnp.broadcast_to(jnp.arange(DIRS, dtype=jnp.int32)[None, :, None], shape3)
    pos_index = jnp.broadcast_to(position, shape3)
    recv_index = jnp.broadcast_to(recv_dom[:, :, None], shape3)
    target = slot_perm[recv_index, dir_index, pos_index]
    sender_index = jnp.broadcast_to(domain_ids[:, None, None], shape3)
    sends = jnp.zeros(shape3, jnp.int32).at[sender_index, dir_index, target].set(values)
    return (near, sends.astype(jnp.int32))


def draw_queries(key, part):
    return jnp.clip(jax.random.normal(jax.random.fold_in(key, 301), (TOKENS, D), jnp.float32), -6.0, 6.0).astype(jnp.bfloat16)


def draw_keys_in(key, part):
    return jnp.clip(jax.random.normal(jax.random.fold_in(key, 302), (TOKENS, D), jnp.float32), -6.0, 6.0).astype(jnp.bfloat16)


def draw_neighbours(key, part):
    return grid_layout(key)[0]


def draw_send_block(key, part):
    return grid_layout(key)[1]


def set_ends(entries, rng, smallest, high):
    extent = entries.shape
    spot = [jax.random.randint(jax.random.fold_in(rng, axis), (), 0, extent[axis]) for axis in range(len(extent))]
    entries = entries.at[tuple(spot)].set(smallest)
    longest = extent.index(max(extent))
    spot[longest] = (spot[longest] + 1) % extent[longest]
    return entries.at[tuple(spot)].set(high)


def block_scale(own_key, shape, cuts, smallest, top_value):
    loudness, own = 1.0, jax.random.fold_in(own_key, 6)
    for dim, blocks in cuts:
        heights = jnp.exp(jax.random.uniform(jax.random.fold_in(own, dim), (blocks,), jnp.float32, smallest / len(cuts), top_value / len(cuts)))
        loudness = loudness * jnp.repeat(heights, shape[dim] // blocks).reshape([-1 if axis == dim else 1 for axis in range(len(shape))])
    return loudness


def normal_values(own_key, shape, scale, bound, cuts=(), kind=jnp.bfloat16):
    loudness = block_scale(own_key, shape, cuts, -0.22, 0.18) if cuts else 1.0
    values = jax.random.normal(own_key, shape, jnp.float32) * scale * loudness
    return jnp.minimum(jnp.maximum(values, -bound), bound).astype(kind)


def setup_inputs(seed: int = 0) -> dict:
    streams_of = jax.random.split(jax.random.key(seed), 9)
    queries = draw_queries(jax.random.fold_in(streams_of[8], 71), 0)
    keys_in = draw_keys_in(jax.random.fold_in(streams_of[8], 71), 0)
    values_in = normal_values(streams_of[2], (TOKENS, D), 1.0, 6.0, ((0, 1024),))
    grad_out = normal_values(streams_of[3], (TOKENS, D), 1.0, 6.0, ((0, 1024),))
    pos_bias = normal_values(streams_of[4], (HEADS, BT, WINK), 0.8, 4.0, ((0, 32),), jnp.float32)
    neighbours = draw_neighbours(jax.random.fold_in(streams_of[8], 71), 0)
    send_block = draw_send_block(jax.random.fold_in(streams_of[8], 71), 0)
    orient = set_ends(jax.random.randint(streams_of[7], (DOMAINS, DIRS), 0, 8), jax.random.fold_in(streams_of[7], 1), 0, 7).astype(jnp.int32)
    return dict(queries=queries, keys_in=keys_in, values_in=values_in, grad_out=grad_out, pos_bias=pos_bias, neighbours=neighbours, send_block=send_block, orient=orient)


def patch_tables(patch_side):
    flat_index = np.arange(patch_side * patch_side)
    row_of = flat_index // patch_side
    col_of = flat_index % patch_side
    table_list = []
    for orient_id in range(8):
        row_new = patch_side - 1 - row_of if orient_id % 2 == 1 else row_of
        col_new = patch_side - 1 - col_of if (orient_id // 2) % 2 == 1 else col_of
        mapped = patch_side * col_new + row_new if orient_id >= 4 else patch_side * row_new + col_new
        table_list.append(mapped)
    forward = np.stack(table_list).astype(np.int32)
    inverse = np.argsort(forward, axis=1).astype(np.int32)
    return forward, inverse


def reference(queries, keys_in, values_in, grad_out, pos_bias, neighbours, send_block, orient):
    forward, inverse = patch_tables(PATCH)
    turn_table = jnp.asarray(forward)
    back_table = jnp.asarray(inverse)
    score_scale = HD ** -0.5
    grid_cols = DOMAINS // GRID_ROWS
    step_rows = jnp.array([-1, -1, -1, 0, 0, 1, 1, 1], jnp.int32)
    step_cols = jnp.array([-1, 0, 1, -1, 1, -1, 0, 1], jnp.int32)
    pairs_all = jnp.concatenate([keys_in.reshape(DOMAINS * QB_DOM, BT, HEADS, HD),
                                 values_in.reshape(DOMAINS * QB_DOM, BT, HEADS, HD)], axis=-1)
    query_all = queries.reshape(DOMAINS, QB_DOM, BT, HEADS, HD)
    grad_all = grad_out.reshape(DOMAINS, QB_DOM, BT, HEADS, HD)
    near_all = neighbours.reshape(DOMAINS, QB_DOM * WIN)
    dir_ids = jnp.arange(DIRS, dtype=jnp.int32)

    def one_domain(totals, domain):
        cell_row = domain // grid_cols
        cell_col = domain % grid_cols
        lender_row = jnp.clip(cell_row + step_rows, 0, GRID_ROWS - 1)
        lender_col = jnp.clip(cell_col + step_cols, 0, grid_cols - 1)
        lender = (lender_row * grid_cols + lender_col).astype(jnp.int32)
        lent = send_block[lender, dir_ids]
        global_ids = (lender[:, None] * QB_DOM + lent).reshape(-1).astype(jnp.int32)
        arrived = pairs_all[global_ids]
        turn_index = jnp.repeat(turn_table[orient[domain]], CAP, axis=0)
        oriented = jnp.take_along_axis(arrived, turn_index[:, :, None, None], axis=1)
        own_ids = (domain * QB_DOM + jnp.arange(QB_DOM, dtype=jnp.int32)).astype(jnp.int32)
        extended = jnp.concatenate([pairs_all[own_ids], oriented], axis=0)
        near_ids = near_all[domain]
        window = extended[near_ids].reshape(QB_DOM, WINK, HEADS, 2 * HD).astype(jnp.float32)
        win_k = window[..., :HD]
        win_v = window[..., HD:]
        query_blk = query_all[domain].astype(jnp.float32)
        grad_blk = grad_all[domain].astype(jnp.float32)
        scores = jnp.einsum('bthd,bkhd->bhtk', query_blk, win_k) * score_scale + pos_bias[None]
        row_top = jnp.max(scores, axis=-1, keepdims=True)
        exp_scores = jnp.exp(scores - row_top)
        probs = exp_scores / jnp.sum(exp_scores, axis=-1, keepdims=True)
        probs_half = probs.astype(jnp.bfloat16)
        probs_wide = lax.optimization_barrier(probs_half).astype(jnp.float32)
        attended = jnp.einsum('bhtk,bkhd->bthd', probs_wide, win_v)
        row_delta = jnp.sum(grad_blk * attended, axis=-1)
        dprobs = jnp.einsum('bthd,bkhd->bhtk', grad_blk, win_v)
        dscores = (probs * (dprobs - jnp.transpose(row_delta, (0, 2, 1))[..., None])).astype(jnp.bfloat16)
        dscores_wide = lax.optimization_barrier(dscores).astype(jnp.float32)
        grad_q_blk = (jnp.einsum('bhtk,bkhd->bthd', dscores_wide, win_k) * score_scale).astype(jnp.bfloat16)
        grad_kw = jnp.einsum('bhtk,bthd->bkhd', dscores_wide, query_blk) * score_scale
        grad_vw = jnp.einsum('bhtk,bthd->bkhd', probs_wide, grad_blk)
        window_grad = jnp.concatenate([grad_kw, grad_vw], axis=-1).reshape(QB_DOM * WIN, BT, HEADS, 2 * HD)
        slot_grad = jax.ops.segment_sum(window_grad, near_ids, num_segments=QB_DOM + DIRS * CAP)
        back_order = jnp.repeat(back_table[orient[domain]], CAP, axis=0)
        returned = jnp.take_along_axis(slot_grad[QB_DOM:], back_order[:, :, None, None], axis=1).astype(jnp.bfloat16)
        returned_wide = lax.optimization_barrier(returned).astype(jnp.float32)
        totals = totals.at[own_ids].add(slot_grad[:QB_DOM])
        totals = totals.at[global_ids].add(returned_wide)
        return totals, grad_q_blk

    start = jnp.zeros((DOMAINS * QB_DOM, BT, HEADS, 2 * HD), jnp.float32)
    totals, grad_q = lax.scan(one_domain, start, jnp.arange(DOMAINS, dtype=jnp.int32))
    grad_q = grad_q.reshape(TOKENS, D)
    grad_k = totals[..., :HD].astype(jnp.bfloat16).reshape(TOKENS, D)
    grad_v = totals[..., HD:].astype(jnp.bfloat16).reshape(TOKENS, D)
    return (grad_q, grad_k, grad_v)
```

```python
import functools

import jax
import jax.numpy as jnp
from jax import lax
from jax.experimental import pallas as pl
from jax.experimental.pallas import tpu as pltpu
from jax.sharding import PartitionSpec as P

HD = 64
LANES = 128
PATCH = 8
BT = 64
GRID_ROWS = 4
DIRS = 8
WIN = 9
QB_DOM = 9
CAP = 3
MAIN = 16
SLOTS = QB_DOM + DIRS * CAP
OFFSETS = [(-1, -1), (-1, 0), (-1, 1), (0, -1), (0, 1), (1, -1), (1, 0), (1, 1)]
MESH = pl.DeviceIdType.MESH
F32 = jnp.float32
BF16 = jnp.bfloat16


def live_slots(row_step, col_step):
    return 1 if row_step and col_step else CAP


def turn_matrix(orient_id):
    token = lax.broadcasted_iota(jnp.int32, (BT, BT), 0)
    target = lax.broadcasted_iota(jnp.int32, (BT, BT), 1)
    r = lax.shift_right_logical(token, 3)
    s = lax.bitwise_and(token, 7)
    flip_r = lax.bitwise_and(orient_id, 1)
    flip_s = lax.bitwise_and(lax.shift_right_logical(orient_id, 1), 1)
    swap = lax.bitwise_and(lax.shift_right_logical(orient_id, 2), 1)
    r2 = r + flip_r * (PATCH - 1 - 2 * r)
    s2 = s + flip_s * (PATCH - 1 - 2 * s)
    mapped = swap * (PATCH * s2 + r2) + (1 - swap) * (PATCH * r2 + s2)
    return jnp.where(target == mapped, 1.0, 0.0).astype(BF16)


def kernel(
    heads, doms,
    near_ref, send_ref, orient_ref, q_ref, k_ref, v_ref, g_ref, bias_ref,
    gq_ref, gk_ref, gv_ref,
    main_out, rest_out, main_in, rest_in,
    pair_rows, qg_rows, ext, staged, arrived, turns,
    window_grads, gq_rows, total_rows, leaving, returned,
    a_out, b_out, c_out, a_in, b_in, c_in,
    inv_near, inv_send,
    in_send, in_recv, dom_send, dom_recv, back_send, back_recv, out_send, out_recv,
):
    grid_cols = doms // GRID_ROWS
    peers = heads - 1
    me = lax.axis_index("head")
    dom = lax.axis_index("dom")
    row = dom // grid_cols
    col = dom % grid_cols
    scale = HD ** (-0.5)

    def inside(r, c):
        return (r >= 0) & (r < GRID_ROWS) & (c >= 0) & (c < grid_cols)

    lender_ok = [inside(row + dr, col + dc) for dr, dc in OFFSETS]
    borrower_ok = [inside(row - dr, col - dc) for dr, dc in OFFSETS]
    lender = [dom + dr * grid_cols + dc for dr, dc in OFFSETS]
    borrower = [dom - dr * grid_cols - dc for dr, dc in OFFSETS]

    def peer_of(n):
        half = (n + 1) // 2
        off = heads // 2 + half * (1 - 2 * (n % 2))
        return (me + off) % heads

    window_grads[:, WIN] = jnp.zeros((QB_DOM, BT, LANES), F32)
    returned[:, CAP] = jnp.zeros((DIRS, BT, LANES), BF16)

    barrier = pltpu.get_barrier_semaphore()

    @pl.loop(0, peers)
    def _(n):
        pl.semaphore_signal(barrier, inc=1, device_id={"head": peer_of(n)}, device_id_type=MESH)

    near_count = jnp.int32(0)
    for kk in range(DIRS):
        near_count = near_count + lender_ok[kk].astype(jnp.int32)

        @pl.when(lender_ok[kk])
        def _():
            pl.semaphore_signal(barrier, inc=1, device_id={"dom": lender[kk]}, device_id_type=MESH)

    def left_half(rows):
        return lax.broadcasted_iota(jnp.int32, (rows, LANES), 1) < HD

    def swap_halves(x):
        return pltpu.roll(x, HD, 1)

    def merge(x, y):
        mask = left_half(x.shape[0])
        return jnp.where(mask, x, swap_halves(y)), jnp.where(mask, swap_halves(x), y)

    @pl.loop(0, heads // 2)
    def _(i):
        cols = pl.ds(pl.multiple_of(i * LANES, LANES), LANES)
        for part, (first, second) in enumerate(((k_ref, v_ref), (q_ref, g_ref))):
            x, y = first[0:MAIN, cols].astype(F32), second[0:MAIN, cols].astype(F32)
            even, odd = merge(x, y)
            main_out[part, 2 * i] = even.astype(BF16)
            main_out[part, 2 * i + 1] = odd.astype(BF16)
            x, y = first[MAIN:, cols].astype(F32), second[MAIN:, cols].astype(F32)
            even, odd = merge(x, y)
            rest_out[part, 2 * i] = even.astype(BF16)
            rest_out[part, 2 * i + 1] = odd.astype(BF16)

    def lent_block(kk, c):
        if live_slots(*OFFSETS[kk]) == CAP:
            return send_ref[0, kk, c]
        return jnp.maximum(jnp.maximum(send_ref[0, kk, 0], send_ref[0, kk, 1]), send_ref[0, kk, 2])

    @pl.loop(0, QB_DOM)
    def _(b):
        names = [near_ref[b, j] for j in range(WIN)]

        def place(first, last):
            at = jnp.int32(WIN)
            for j in range(WIN):
                at = jnp.where((names[j] >= first) & (names[j] <= last), j, at)
            return at

        for e in range(QB_DOM):
            inv_near[b, e] = place(e, e)
        for kk, step in enumerate(OFFSETS):
            live = live_slots(*step)
            for c in range(live):
                e = QB_DOM + kk * CAP + c
                inv_near[b, e] = place(e, e + CAP - live)
        for kk, step in enumerate(OFFSETS):
            at = jnp.int32(CAP)
            for c in range(live_slots(*step)):
                at = jnp.where(borrower_ok[kk] & (lent_block(kk, c) == b), c, at)
            inv_send[b, kk] = at

    for kk in range(DIRS):
        turns[kk] = turn_matrix(orient_ref[0, kk])

    pl.semaphore_wait(barrier, peers + near_count)

    def to_peer(src, dst, sem, peer):
        return pltpu.make_async_remote_copy(
            src_ref=src, dst_ref=dst, send_sem=in_send.at[sem], recv_sem=in_recv.at[sem],
            device_id={"head": peer}, device_id_type=MESH,
        )

    for part in range(2):

        @pl.loop(0, peers)
        def _(n):
            peer = peer_of(n)
            to_peer(main_out.at[part, peer], main_in.at[part, me], 2 * part, peer).start()
            to_peer(rest_out.at[part, peer], rest_in.at[part, me], 2 * part + 1, peer).start()

        main_in[part, me] = main_out[part, me]
        rest_in[part, me] = rest_out[part, me]

    some = pl.ds(0, peers)

    def unpack_rows(part, rows):
        to_peer(main_out.at[part, some], main_in.at[part, some], 2 * part, peer_of(0)).wait_recv()
        to_peer(rest_out.at[part, some], rest_in.at[part, some], 2 * part + 1, peer_of(0)).wait_recv()
        count = MAIN + rest_in.shape[2]
        for source in range(heads):
            base = source * count
            rows[base:base + MAIN] = main_in[part, source].astype(F32)
            rows[base + MAIN:base + count] = rest_in[part, source].astype(F32)

    unpack_rows(0, pair_rows)
    for b in range(QB_DOM):
        ext[b] = pair_rows[b * BT:(b + 1) * BT].astype(BF16)

    def lend(kk):
        live = pl.ds(0, live_slots(*OFFSETS[kk]))
        return pltpu.make_async_remote_copy(
            src_ref=staged.at[kk, live], dst_ref=arrived.at[kk, live],
            send_sem=dom_send.at[kk], recv_sem=dom_recv.at[kk],
            device_id={"dom": borrower[kk]}, device_id_type=MESH,
        )

    for kk, step in enumerate(OFFSETS):
        for c in range(live_slots(*step)):
            staged[kk, c] = ext[lent_block(kk, c)]
    for kk in range(DIRS):

        @pl.when(borrower_ok[kk])
        def _():
            lend(kk).start()

    unpack_rows(1, qg_rows)

    for kk, step in enumerate(OFFSETS):

        @pl.when(lender_ok[kk])
        def _():
            lend(kk).wait_recv()
            for c in range(live_slots(*step)):
                turned = jnp.dot(turns[kk], arrived[kk, c], preferred_element_type=F32).astype(BF16)
                for same in range(c, c + 1 + CAP - live_slots(*step)):
                    ext[QB_DOM + kk * CAP + same] = turned

    lane = lax.broadcasted_iota(jnp.int32, (1, LANES), 1)
    pair_scale = jnp.where(lane < HD, scale, 1.0).astype(F32)

    @pl.loop(0, QB_DOM)
    def _(b):
        rows = pl.ds(pl.multiple_of(b * BT, BT), BT)
        qg = qg_rows[rows]
        mask = left_half(BT)
        qg2 = jnp.concatenate([jnp.where(mask, qg, 0.0), jnp.where(mask, 0.0, qg)], axis=0).astype(BF16)
        window = jnp.concatenate([ext[near_ref[b, j]] for j in range(WIN)], axis=0)
        both = lax.dot_general(qg2, window, (((1,), (1,)), ((), ())), preferred_element_type=F32)
        scores = both[:BT] * scale + bias_ref[0]
        dprobs = both[BT:]
        top = jnp.max(scores, axis=1, keepdims=True)
        exps = jnp.exp(scores - top)
        probs = exps / jnp.sum(exps, axis=1, keepdims=True)
        half = probs.astype(BF16)
        delta = jnp.sum(half.astype(F32) * dprobs, axis=1, keepdims=True)
        dscores = (probs * (dprobs - delta)).astype(BF16)
        gq_rows[rows] = jnp.dot(dscores, window, preferred_element_type=F32) * scale
        stacked = jnp.concatenate([dscores, half], axis=0)
        grads = lax.dot_general(stacked, qg2, (((0,), (0,)), ((), ())), preferred_element_type=F32)
        grads = grads * pair_scale
        for j in range(WIN):
            window_grads[b, j] = grads[j * BT:(j + 1) * BT]

    def slot_grad(e):
        acc = window_grads[0, inv_near[0, e]]
        for b in range(1, QB_DOM):
            acc = acc + window_grads[b, inv_near[b, e]]
        return acc

    def give_back(kk):
        live = pl.ds(0, live_slots(*OFFSETS[kk]))
        return pltpu.make_async_remote_copy(
            src_ref=leaving.at[kk, live], dst_ref=returned.at[kk, live],
            send_sem=back_send.at[kk], recv_sem=back_recv.at[kk],
            device_id={"dom": lender[kk]}, device_id_type=MESH,
        )

    for kk, step in enumerate(OFFSETS):

        @pl.when(lender_ok[kk])
        def _():
            for c in range(live_slots(*step)):
                leaving[kk, c] = lax.dot_general(
                    turns[kk], slot_grad(QB_DOM + kk * CAP + c).astype(BF16),
                    (((0,), (0,)), ((), ())), preferred_element_type=F32,
                ).astype(BF16)

    for kk in range(DIRS):

        @pl.when(lender_ok[kk])
        def _():
            give_back(kk).start()

    def home(src, dst, sem, peer):
        return pltpu.make_async_remote_copy(
            src_ref=src, dst_ref=dst, send_sem=out_send.at[sem], recv_sem=out_recv.at[sem],
            device_id={"head": peer}, device_id_type=MESH,
        )

    count = MAIN + rest_in.shape[2]
    half_main = MAIN // 2
    for peer in range(heads):
        base = peer * count
        first = gq_rows[base:base + half_main]
        second = gq_rows[base + half_main:base + MAIN]
        a_out[peer] = jnp.where(left_half(half_main), first, swap_halves(second)).astype(BF16)

    @pl.loop(0, peers)
    def _(n):
        peer = peer_of(n)
        home(a_out.at[peer], a_in.at[me], 0, peer).start()

    a_in[me] = a_out[me]

    for b in range(QB_DOM):
        total_rows[b * BT:(b + 1) * BT] = slot_grad(b)

    for kk in range(DIRS):

        @pl.when(borrower_ok[kk])
        def _():
            give_back(kk).wait_recv()

    for b in range(QB_DOM):
        acc = total_rows[b * BT:(b + 1) * BT]
        for kk in range(DIRS):
            acc = acc + returned[kk, inv_send[b, kk]].astype(F32)
        total_rows[b * BT:(b + 1) * BT] = acc

    for peer in range(heads):
        base = peer * count
        b_out[peer] = total_rows[base:base + MAIN].astype(BF16)
        rest = total_rows[base + MAIN:base + count]
        c_out[peer, 0:2] = rest.astype(BF16)
        rest = gq_rows[base + MAIN:base + count]
        c_out[peer, 2:4] = rest.astype(BF16)

    @pl.loop(0, peers)
    def _(n):
        peer = peer_of(n)
        home(b_out.at[peer], b_in.at[me], 1, peer).start()
        home(c_out.at[peer], c_in.at[me], 2, peer).start()

    b_in[me] = b_out[me]
    c_in[me] = c_out[me]

    home(a_out.at[some], a_in.at[some], 0, peer_of(0)).wait_recv()
    home(b_out.at[some], b_in.at[some], 1, peer_of(0)).wait_recv()
    home(c_out.at[some], c_in.at[some], 2, peer_of(0)).wait_recv()

    @pl.loop(0, heads // 2)
    def _(i):
        cols = pl.ds(pl.multiple_of(i * LANES, LANES), LANES)
        x, y = a_in[2 * i].astype(F32), a_in[2 * i + 1].astype(F32)
        mask = left_half(half_main)
        gq_ref[0:half_main, cols] = jnp.where(mask, x, swap_halves(y)).astype(BF16)
        gq_ref[half_main:MAIN, cols] = jnp.where(mask, swap_halves(x), y).astype(BF16)
        x, y = b_in[2 * i].astype(F32), b_in[2 * i + 1].astype(F32)
        mask = left_half(MAIN)
        gk_ref[0:MAIN, cols] = jnp.where(mask, x, swap_halves(y)).astype(BF16)
        gv_ref[0:MAIN, cols] = jnp.where(mask, swap_halves(x), y).astype(BF16)
        x, y = c_in[2 * i].astype(F32), c_in[2 * i + 1].astype(F32)
        mask = left_half(4)
        front = jnp.where(mask, x, swap_halves(y))
        gk_ref[MAIN:count, cols] = front[0:2].astype(BF16)
        gq_ref[MAIN:count, cols] = front[2:4].astype(BF16)
        back = jnp.where(mask, swap_halves(x), y)
        gv_ref[MAIN:count, cols] = back[0:2].astype(BF16)

    for part in range(2):
        to_peer(main_out.at[part, some], main_in.at[part, some], 2 * part, peer_of(0)).wait_send()
        to_peer(rest_out.at[part, some], rest_in.at[part, some], 2 * part + 1, peer_of(0)).wait_send()
    for kk in range(DIRS):

        @pl.when(borrower_ok[kk])
        def _():
            lend(kk).wait_send()

        @pl.when(lender_ok[kk])
        def _():
            give_back(kk).wait_send()

    home(a_out.at[some], a_in.at[some], 0, peer_of(0)).wait_send()
    home(b_out.at[some], b_in.at[some], 1, peer_of(0)).wait_send()
    home(c_out.at[some], c_in.at[some], 2, peer_of(0)).wait_send()


def per_device(heads, doms, queries, keys_in, values_in, grad_out, pos_bias, neighbours, send_block, orient):
    rows, width = queries.shape
    rest = rows - MAIN
    tokens = QB_DOM * BT
    whole = pl.BlockSpec(memory_space=pltpu.VMEM)
    small = pl.BlockSpec(memory_space=pltpu.SMEM)
    out = jax.ShapeDtypeStruct((rows, width), BF16)
    block = (BT, LANES)
    dma = pltpu.SemaphoreType.DMA
    return pl.pallas_call(
        functools.partial(kernel, heads, doms),
        out_shape=(out, out, out),
        in_specs=[small] * 3 + [whole] * 5,
        out_specs=(whole, whole, whole),
        scratch_shapes=[
            pltpu.VMEM((2, heads, MAIN, LANES), BF16),
            pltpu.VMEM((2, heads, rest, LANES), BF16),
            pltpu.VMEM((2, heads, MAIN, LANES), BF16),
            pltpu.VMEM((2, heads, rest, LANES), BF16),
            pltpu.VMEM((tokens, LANES), F32),
            pltpu.VMEM((tokens, LANES), F32),
            pltpu.VMEM((SLOTS,) + block, BF16),
            pltpu.VMEM((DIRS, CAP) + block, BF16),
            pltpu.VMEM((DIRS, CAP) + block, BF16),
            pltpu.VMEM((DIRS, BT, BT), BF16),
            pltpu.VMEM((QB_DOM, WIN + 1) + block, F32),
            pltpu.VMEM((tokens, LANES), F32),
            pltpu.VMEM((tokens, LANES), F32),
            pltpu.VMEM((DIRS, CAP) + block, BF16),
            pltpu.VMEM((DIRS, CAP + 1) + block, BF16),
            pltpu.VMEM((heads, MAIN // 2, LANES), BF16),
            pltpu.VMEM((heads, MAIN, LANES), BF16),
            pltpu.VMEM((heads, 2 * rest, LANES), BF16),
            pltpu.VMEM((heads, MAIN // 2, LANES), BF16),
            pltpu.VMEM((heads, MAIN, LANES), BF16),
            pltpu.VMEM((heads, 2 * rest, LANES), BF16),
            pltpu.SMEM((QB_DOM, SLOTS), jnp.int32),
            pltpu.SMEM((QB_DOM, DIRS), jnp.int32),
            dma((4,)), dma((4,)),
            dma((DIRS,)), dma((DIRS,)),
            dma((DIRS,)), dma((DIRS,)),
            dma((3,)), dma((3,)),
        ],
        compiler_params=pltpu.CompilerParams(collective_id=0, has_side_effects=True),
    )(neighbours, send_block, orient, queries, keys_in, values_in, grad_out, pos_bias)


def solution(mesh):
    both = P(("dom", "head"), None)
    return jax.shard_map(
        functools.partial(per_device, mesh.shape["head"], mesh.shape["dom"]),
        mesh=mesh,
        in_specs=(both, both, both, both, P("head", None, None), P("dom", None), P("dom", None, None), P("dom", None)),
        out_specs=(both, both, both),
        check_vma=False,
    )
```

```python
import functools

import jax
import jax.numpy as jnp
from jax import lax
from jax.experimental import pallas as pl
from jax.experimental.pallas import tpu as pltpu
from jax.sharding import PartitionSpec as P

HD = 64
LANES = 128
PATCH = 8
BT = 64
GRID_ROWS = 4
DIRS = 8
WIN = 9
QB_DOM = 9
CAP = 3
MAIN = 16
SLOTS = QB_DOM + DIRS * CAP
OFFSETS = [(-1, -1), (-1, 0), (-1, 1), (0, -1), (0, 1), (1, -1), (1, 0), (1, 1)]
MESH = pl.DeviceIdType.MESH
F32 = jnp.float32
BF16 = jnp.bfloat16


def live_slots(row_step, col_step):
    return 1 if row_step and col_step else CAP


def turn_matrix(orient_id):
    token = lax.broadcasted_iota(jnp.int32, (BT, BT), 0)
    target = lax.broadcasted_iota(jnp.int32, (BT, BT), 1)
    r = lax.shift_right_logical(token, 3)
    s = lax.bitwise_and(token, 7)
    flip_r = lax.bitwise_and(orient_id, 1)
    flip_s = lax.bitwise_and(lax.shift_right_logical(orient_id, 1), 1)
    swap = lax.bitwise_and(lax.shift_right_logical(orient_id, 2), 1)
    r2 = r + flip_r * (PATCH - 1 - 2 * r)
    s2 = s + flip_s * (PATCH - 1 - 2 * s)
    mapped = swap * (PATCH * s2 + r2) + (1 - swap) * (PATCH * r2 + s2)
    return jnp.where(target == mapped, 1.0, 0.0).astype(BF16)


def kernel(
    heads, doms,
    near_ref, send_ref, orient_ref, q_any, k_any, v_any, g_any, bias_any,
    gq_ref, gk_ref, gv_ref,
    q_ref, k_ref, v_ref, g_ref, bias_ref,
    main_out, rest_out, main_in, rest_in,
    pair_rows, qg_rows, ext, staged, arrived, turns,
    window_grads, gq_rows, total_rows, leaving, returned,
    a_out, b_out, c_out, a_in, b_in, c_in,
    inv_near, inv_send,
    load_sem, right_sem, left_sem,
    in_send, in_recv, dom_send, dom_recv, back_send, back_recv, out_send, out_recv,
):
    grid_cols = doms // GRID_ROWS
    peers = heads - 1
    me = lax.axis_index("head")
    dom = lax.axis_index("dom")
    row = dom // grid_cols
    col = dom % grid_cols
    scale = HD ** (-0.5)

    def inside(r, c):
        return (r >= 0) & (r < GRID_ROWS) & (c >= 0) & (c < grid_cols)

    lender_ok = [inside(row + dr, col + dc) for dr, dc in OFFSETS]
    borrower_ok = [inside(row - dr, col - dc) for dr, dc in OFFSETS]
    lender = [dom + dr * grid_cols + dc for dr, dc in OFFSETS]
    borrower = [dom - dr * grid_cols - dc for dr, dc in OFFSETS]

    def peer_of(n):
        half = (n + 1) // 2
        off = heads // 2 + half * (1 - 2 * (n % 2))
        return (me + off) % heads

    right, left = (me + 1) % heads, (me + peers) % heads
    far = heads // 2

    returned[:, CAP] = jnp.zeros((DIRS, BT, LANES), BF16)

    barrier = pltpu.get_barrier_semaphore()
    near_count = jnp.int32(2)
    for side in (right, left):
        pl.semaphore_signal(barrier, inc=1, device_id={"head": side}, device_id_type=MESH)
    for kk in range(DIRS):
        near_count = near_count + lender_ok[kk].astype(jnp.int32)

        @pl.when(lender_ok[kk])
        def _():
            pl.semaphore_signal(barrier, inc=1, device_id={"dom": lender[kk]}, device_id_type=MESH)

    pairs = ((k_any, k_ref), (v_any, v_ref), (q_any, q_ref), (g_any, g_ref), (bias_any, bias_ref))
    loads = [pltpu.make_async_copy(src, dst, load_sem.at[n]) for n, (src, dst) in enumerate(pairs)]
    for load in loads:
        load.start()

    def left_half(rows):
        return lax.broadcasted_iota(jnp.int32, (rows, LANES), 1) < HD

    def swap_halves(x):
        return pltpu.roll(x, HD, 1)

    def merge(x, y):
        mask = left_half(x.shape[0])
        return jnp.where(mask, x, swap_halves(y)), jnp.where(mask, swap_halves(x), y)

    def pack(part, first, second):
        for i in range(heads // 2):
            cols = slice(i * LANES, (i + 1) * LANES)
            x, y = first[0:MAIN, cols].astype(F32), second[0:MAIN, cols].astype(F32)
            even, odd = merge(x, y)
            main_out[part, 2 * i] = even.astype(BF16)
            main_out[part, 2 * i + 1] = odd.astype(BF16)
            x, y = first[MAIN:, cols].astype(F32), second[MAIN:, cols].astype(F32)
            even, odd = merge(x, y)
            rest_out[part, 2 * i] = even.astype(BF16)
            rest_out[part, 2 * i + 1] = odd.astype(BF16)
        main_in[part, me] = main_out[part, me]
        rest_in[part, me] = rest_out[part, me]

    def to_peer(src, dst, sem, peer):
        return pltpu.make_async_remote_copy(
            src_ref=src, dst_ref=dst, send_sem=in_send.at[sem], recv_sem=in_recv.at[sem],
            device_id={"head": peer}, device_id_type=MESH,
        )

    def send_rows(part, peer):
        to_peer(main_out.at[part, peer], main_in.at[part, me], 2 * part, peer).start()
        to_peer(rest_out.at[part, peer], rest_in.at[part, me], 2 * part + 1, peer).start()

    loads[0].wait()
    loads[1].wait()
    pack(0, k_ref, v_ref)

    pl.semaphore_wait(barrier, near_count)

    def pass_on(m):
        pl.semaphore_signal(right_sem.at[m + 1], inc=1, device_id={"head": left}, device_id_type=MESH)

        @pl.when(m + 1 < far)
        def _():
            pl.semaphore_signal(left_sem.at[m + 1], inc=1, device_id={"head": right}, device_id_type=MESH)

    pass_on(1)
    send_rows(0, right)
    send_rows(0, left)

    @pl.loop(2, far)
    def _(m):
        pl.semaphore_wait(right_sem.at[m], 1)
        pl.semaphore_wait(left_sem.at[m], 1)
        pass_on(m)
        send_rows(0, (me + m) % heads)
        send_rows(0, (me + heads - m) % heads)

    loads[2].wait()
    loads[3].wait()
    pack(1, q_ref, g_ref)
    pl.semaphore_wait(right_sem.at[far], 1)
    send_rows(0, (me + far) % heads)

    @pl.loop(0, peers)
    def _(n):
        send_rows(1, peer_of(n))

    window_grads[:, WIN] = jnp.zeros((QB_DOM, BT, LANES), F32)

    def lent_block(kk, c):
        if live_slots(*OFFSETS[kk]) == CAP:
            return send_ref[c, 0, kk]
        return jnp.maximum(jnp.maximum(send_ref[0, 0, kk], send_ref[1, 0, kk]), send_ref[2, 0, kk])

    @pl.loop(0, QB_DOM)
    def _(b):
        names = [near_ref[b, j] for j in range(WIN)]

        def place(first, last):
            at = jnp.int32(WIN)
            for j in range(WIN):
                at = jnp.where((names[j] >= first) & (names[j] <= last), j, at)
            return at

        for e in range(QB_DOM):
            inv_near[b, e] = place(e, e)
        for kk, step in enumerate(OFFSETS):
            live = live_slots(*step)
            for c in range(live):
                e = QB_DOM + kk * CAP + c
                inv_near[b, e] = place(e, e + CAP - live)
        for kk, step in enumerate(OFFSETS):
            at = jnp.int32(CAP)
            for c in range(live_slots(*step)):
                at = jnp.where(borrower_ok[kk] & (lent_block(kk, c) == b), c, at)
            inv_send[b, kk] = at

    for kk in range(DIRS):
        turns[kk] = turn_matrix(orient_ref[0, kk])

    some = pl.ds(0, peers)

    def unpack_rows(part, rows):
        to_peer(main_out.at[part, some], main_in.at[part, some], 2 * part, peer_of(0)).wait_recv()
        to_peer(rest_out.at[part, some], rest_in.at[part, some], 2 * part + 1, peer_of(0)).wait_recv()
        count = MAIN + rest_in.shape[2]
        for source in range(heads):
            base = source * count
            rows[base:base + MAIN] = main_in[part, source].astype(F32)
            rows[base + MAIN:base + count] = rest_in[part, source].astype(F32)

    unpack_rows(0, pair_rows)
    for b in range(QB_DOM):
        ext[b] = pair_rows[b * BT:(b + 1) * BT].astype(BF16)

    def lend(kk):
        live = pl.ds(0, live_slots(*OFFSETS[kk]))
        return pltpu.make_async_remote_copy(
            src_ref=staged.at[kk, live], dst_ref=arrived.at[kk, live],
            send_sem=dom_send.at[kk], recv_sem=dom_recv.at[kk],
            device_id={"dom": borrower[kk]}, device_id_type=MESH,
        )

    for kk, step in enumerate(OFFSETS):
        for c in range(live_slots(*step)):
            staged[kk, c] = ext[lent_block(kk, c)]
    for kk in range(DIRS):

        @pl.when(borrower_ok[kk])
        def _():
            lend(kk).start()

    unpack_rows(1, qg_rows)

    for kk, step in enumerate(OFFSETS):

        @pl.when(lender_ok[kk])
        def _():
            lend(kk).wait_recv()
            for c in range(live_slots(*step)):
                turned = jnp.dot(turns[kk], arrived[kk, c], preferred_element_type=F32).astype(BF16)
                for same in range(c, c + 1 + CAP - live_slots(*step)):
                    ext[QB_DOM + kk * CAP + same] = turned

    loads[4].wait()
    lane = lax.broadcasted_iota(jnp.int32, (1, LANES), 1)
    pair_scale = jnp.where(lane < HD, scale, 1.0).astype(F32)

    for b in range(QB_DOM):
        rows = slice(b * BT, (b + 1) * BT)
        qg = qg_rows[rows]
        mask = left_half(BT)
        qg2 = jnp.concatenate([jnp.where(mask, qg, 0.0), jnp.where(mask, 0.0, qg)], axis=0).astype(BF16)
        window = jnp.concatenate([ext[near_ref[b, j]] for j in range(WIN)], axis=0)
        both = lax.dot_general(qg2, window, (((1,), (1,)), ((), ())), preferred_element_type=F32)
        scores = both[:BT] * scale + bias_ref[0]
        dprobs = both[BT:]
        top = jnp.max(scores, axis=1, keepdims=True)
        exps = jnp.exp(scores - top)
        probs = exps / jnp.sum(exps, axis=1, keepdims=True)
        half = probs.astype(BF16)
        delta = jnp.sum(half.astype(F32) * dprobs, axis=1, keepdims=True)
        dscores = (probs * (dprobs - delta)).astype(BF16)
        gq_rows[rows] = jnp.dot(dscores, window, preferred_element_type=F32) * scale
        stacked = jnp.concatenate([dscores, half], axis=0)
        grads = lax.dot_general(stacked, qg2, (((0,), (0,)), ((), ())), preferred_element_type=F32)
        grads = grads * pair_scale
        for j in range(WIN):
            window_grads[b, j] = grads[j * BT:(j + 1) * BT]

    def slot_grad(e):
        acc = window_grads[0, inv_near[0, e]]
        for b in range(1, QB_DOM):
            acc = acc + window_grads[b, inv_near[b, e]]
        return acc

    def give_back(kk):
        live = pl.ds(0, live_slots(*OFFSETS[kk]))
        return pltpu.make_async_remote_copy(
            src_ref=leaving.at[kk, live], dst_ref=returned.at[kk, live],
            send_sem=back_send.at[kk], recv_sem=back_recv.at[kk],
            device_id={"dom": lender[kk]}, device_id_type=MESH,
        )

    for kk, step in enumerate(OFFSETS):

        @pl.when(lender_ok[kk])
        def _():
            for c in range(live_slots(*step)):
                leaving[kk, c] = lax.dot_general(
                    turns[kk], slot_grad(QB_DOM + kk * CAP + c).astype(BF16),
                    (((0,), (0,)), ((), ())), preferred_element_type=F32,
                ).astype(BF16)

    for kk in range(DIRS):

        @pl.when(lender_ok[kk])
        def _():
            give_back(kk).start()

    def home(src, dst, sem, peer):
        return pltpu.make_async_remote_copy(
            src_ref=src, dst_ref=dst, send_sem=out_send.at[sem], recv_sem=out_recv.at[sem],
            device_id={"head": peer}, device_id_type=MESH,
        )

    count = MAIN + rest_in.shape[2]
    half_main = MAIN // 2
    for peer in range(heads):
        base = peer * count
        first = gq_rows[base:base + half_main]
        second = gq_rows[base + half_main:base + MAIN]
        a_out[peer] = jnp.where(left_half(half_main), first, swap_halves(second)).astype(BF16)

    @pl.loop(0, peers)
    def _(n):
        peer = peer_of(n)
        home(a_out.at[peer], a_in.at[me], 0, peer).start()

    a_in[me] = a_out[me]

    for b in range(QB_DOM):
        total_rows[b * BT:(b + 1) * BT] = slot_grad(b)

    for kk in range(DIRS):

        @pl.when(borrower_ok[kk])
        def _():
            give_back(kk).wait_recv()

    for b in range(QB_DOM):
        acc = total_rows[b * BT:(b + 1) * BT]
        for kk in range(DIRS):
            acc = acc + returned[kk, inv_send[b, kk]].astype(F32)
        total_rows[b * BT:(b + 1) * BT] = acc

    for peer in range(heads):
        base = peer * count
        b_out[peer] = total_rows[base:base + MAIN].astype(BF16)
        rest = total_rows[base + MAIN:base + count]
        c_out[peer, 0:2] = rest.astype(BF16)
        rest = gq_rows[base + MAIN:base + count]
        c_out[peer, 2:4] = rest.astype(BF16)

    @pl.loop(0, peers)
    def _(n):
        peer = peer_of(n)
        home(b_out.at[peer], b_in.at[me], 1, peer).start()
        home(c_out.at[peer], c_in.at[me], 2, peer).start()

    b_in[me] = b_out[me]
    c_in[me] = c_out[me]

    home(a_out.at[some], a_in.at[some], 0, peer_of(0)).wait_recv()
    home(b_out.at[some], b_in.at[some], 1, peer_of(0)).wait_recv()
    home(c_out.at[some], c_in.at[some], 2, peer_of(0)).wait_recv()

    @pl.loop(0, heads // 2)
    def _(i):
        cols = pl.ds(pl.multiple_of(i * LANES, LANES), LANES)
        x, y = a_in[2 * i].astype(F32), a_in[2 * i + 1].astype(F32)
        mask = left_half(half_main)
        gq_ref[0:half_main, cols] = jnp.where(mask, x, swap_halves(y)).astype(BF16)
        gq_ref[half_main:MAIN, cols] = jnp.where(mask, swap_halves(x), y).astype(BF16)
        x, y = b_in[2 * i].astype(F32), b_in[2 * i + 1].astype(F32)
        mask = left_half(MAIN)
        gk_ref[0:MAIN, cols] = jnp.where(mask, x, swap_halves(y)).astype(BF16)
        gv_ref[0:MAIN, cols] = jnp.where(mask, swap_halves(x), y).astype(BF16)
        x, y = c_in[2 * i].astype(F32), c_in[2 * i + 1].astype(F32)
        mask = left_half(4)
        front = jnp.where(mask, x, swap_halves(y))
        gk_ref[MAIN:count, cols] = front[0:2].astype(BF16)
        gq_ref[MAIN:count, cols] = front[2:4].astype(BF16)
        back = jnp.where(mask, swap_halves(x), y)
        gv_ref[MAIN:count, cols] = back[0:2].astype(BF16)

    for part in range(2):
        to_peer(main_out.at[part, some], main_in.at[part, some], 2 * part, peer_of(0)).wait_send()
        to_peer(rest_out.at[part, some], rest_in.at[part, some], 2 * part + 1, peer_of(0)).wait_send()
    for kk in range(DIRS):

        @pl.when(borrower_ok[kk])
        def _():
            lend(kk).wait_send()

        @pl.when(lender_ok[kk])
        def _():
            give_back(kk).wait_send()

    home(a_out.at[some], a_in.at[some], 0, peer_of(0)).wait_send()
    home(b_out.at[some], b_in.at[some], 1, peer_of(0)).wait_send()
    home(c_out.at[some], c_in.at[some], 2, peer_of(0)).wait_send()


def per_device(heads, doms, queries, keys_in, values_in, grad_out, pos_bias, neighbours, send_block, orient):
    rows, width = queries.shape
    rest = rows - MAIN
    tokens = QB_DOM * BT
    whole = pl.BlockSpec(memory_space=pltpu.VMEM)
    small = pl.BlockSpec(memory_space=pltpu.SMEM)
    out = jax.ShapeDtypeStruct((rows, width), BF16)
    block = (BT, LANES)
    dma = pltpu.SemaphoreType.DMA
    return pl.pallas_call(
        functools.partial(kernel, heads, doms),
        out_shape=(out, out, out),
        in_specs=[small] * 3 + [pl.BlockSpec(memory_space=pl.ANY)] * 5,
        out_specs=(whole, whole, whole),
        scratch_shapes=[
            *[pltpu.VMEM((rows, width), BF16)] * 4,
            pltpu.VMEM(pos_bias.shape, F32),
            pltpu.VMEM((2, heads, MAIN, LANES), BF16),
            pltpu.VMEM((2, heads, rest, LANES), BF16),
            pltpu.VMEM((2, heads, MAIN, LANES), BF16),
            pltpu.VMEM((2, heads, rest, LANES), BF16),
            pltpu.VMEM((tokens, LANES), F32),
            pltpu.VMEM((tokens, LANES), F32),
            pltpu.VMEM((SLOTS,) + block, BF16),
            pltpu.VMEM((DIRS, CAP) + block, BF16),
            pltpu.VMEM((DIRS, CAP) + block, BF16),
            pltpu.VMEM((DIRS, BT, BT), BF16),
            pltpu.VMEM((QB_DOM, WIN + 1) + block, F32),
            pltpu.VMEM((tokens, LANES), F32),
            pltpu.VMEM((tokens, LANES), F32),
            pltpu.VMEM((DIRS, CAP) + block, BF16),
            pltpu.VMEM((DIRS, CAP + 1) + block, BF16),
            pltpu.VMEM((heads, MAIN // 2, LANES), BF16),
            pltpu.VMEM((heads, MAIN, LANES), BF16),
            pltpu.VMEM((heads, 2 * rest, LANES), BF16),
            pltpu.VMEM((heads, MAIN // 2, LANES), BF16),
            pltpu.VMEM((heads, MAIN, LANES), BF16),
            pltpu.VMEM((heads, 2 * rest, LANES), BF16),
            pltpu.SMEM((QB_DOM, SLOTS), jnp.int32),
            pltpu.SMEM((QB_DOM, DIRS), jnp.int32),
            dma((5,)),
            pltpu.SemaphoreType.REGULAR((heads // 2 + 1,)),
            pltpu.SemaphoreType.REGULAR((heads // 2 + 1,)),
            dma((4,)), dma((4,)),
            dma((DIRS,)), dma((DIRS,)),
            dma((DIRS,)), dma((DIRS,)),
            dma((3,)), dma((3,)),
        ],
        compiler_params=pltpu.CompilerParams(collective_id=0, has_side_effects=True),
    )(neighbours, jnp.transpose(send_block, (2, 0, 1)), orient, queries, keys_in, values_in, grad_out, pos_bias)


def solution(mesh):
    both = P(("dom", "head"), None)
    return jax.shard_map(
        functools.partial(per_device, mesh.shape["head"], mesh.shape["dom"]),
        mesh=mesh,
        in_specs=(both, both, both, both, P("head", None, None), P("dom", None), P("dom", None, None), P("dom", None)),
        out_specs=(both, both, both),
        check_vma=False,
    )
```

```python
import functools

import jax
import jax.numpy as jnp
from jax import lax
from jax.experimental import pallas as pl
from jax.experimental.pallas import tpu as pltpu
from jax.sharding import PartitionSpec as P

HD = 64
LANES = 128
PATCH = 8
BT = 64
GRID_ROWS = 4
DIRS = 8
WIN = 9
QB_DOM = 9
CAP = 3
MAIN = 16
SLOTS = QB_DOM + DIRS * CAP
OFFSETS = [(-1, -1), (-1, 0), (-1, 1), (0, -1), (0, 1), (1, -1), (1, 0), (1, 1)]
MESH = pl.DeviceIdType.MESH
F32 = jnp.float32
BF16 = jnp.bfloat16


def live_slots(row_step, col_step):
    return 1 if row_step and col_step else CAP


def turn_matrix(orient_id):
    token = lax.broadcasted_iota(jnp.int32, (BT, BT), 0)
    target = lax.broadcasted_iota(jnp.int32, (BT, BT), 1)
    r = lax.shift_right_logical(token, 3)
    s = lax.bitwise_and(token, 7)
    flip_r = lax.bitwise_and(orient_id, 1)
    flip_s = lax.bitwise_and(lax.shift_right_logical(orient_id, 1), 1)
    swap = lax.bitwise_and(lax.shift_right_logical(orient_id, 2), 1)
    r2 = r + flip_r * (PATCH - 1 - 2 * r)
    s2 = s + flip_s * (PATCH - 1 - 2 * s)
    mapped = swap * (PATCH * s2 + r2) + (1 - swap) * (PATCH * r2 + s2)
    return jnp.where(target == mapped, 1.0, 0.0).astype(BF16)


def left_half(rows):
    return lax.broadcasted_iota(jnp.int32, (rows, LANES), 1) < HD


def swap_halves(x):
    return pltpu.roll(x, HD, 1)


def merge(x, y):
    mask = left_half(x.shape[0])
    return jnp.where(mask, x, swap_halves(y)), jnp.where(mask, swap_halves(x), y)


def lay_out(a_ref, b_ref, c_ref, gq_ref, gk_ref, gv_ref):
    heads, half_main = a_ref.shape[:2]
    rest = c_ref.shape[1] // 2
    for i in range(heads // 2):
        cols = slice(i * LANES, (i + 1) * LANES)
        first, second = merge(a_ref[2 * i].astype(F32), a_ref[2 * i + 1].astype(F32))
        gq_ref[0:half_main, cols] = first.astype(BF16)
        gq_ref[half_main:MAIN, cols] = second.astype(BF16)
        first, second = merge(b_ref[2 * i].astype(F32), b_ref[2 * i + 1].astype(F32))
        gk_ref[0:MAIN, cols] = first.astype(BF16)
        gv_ref[0:MAIN, cols] = second.astype(BF16)
        first, second = merge(c_ref[2 * i].astype(F32), c_ref[2 * i + 1].astype(F32))
        gk_ref[MAIN:, cols] = first[0:rest].astype(BF16)
        gq_ref[MAIN:, cols] = first[rest:].astype(BF16)
        gv_ref[MAIN:, cols] = second[0:rest].astype(BF16)


def kernel(
    heads, doms,
    near_ref, send_ref, orient_ref, q_any, k_any, v_any, g_any, bias_any,
    a_in, b_in, c_in,
    q_ref, k_ref, v_ref, g_ref, bias_ref,
    main_out, rest_out, main_in, rest_in,
    pair_rows, qg_rows, ext, staged, arrived, turns,
    window_grads, gq_rows, total_rows, leaving, returned,
    a_out, b_out, c_out,
    inv_near, inv_send,
    load_sem, keep_sem,
    in_send, in_recv, dom_send, dom_recv, back_send, back_recv, out_send, out_recv,
):
    grid_cols = doms // GRID_ROWS
    peers = heads - 1
    me = lax.axis_index("head")
    dom = lax.axis_index("dom")
    row = dom // grid_cols
    col = dom % grid_cols
    scale = HD ** (-0.5)

    def inside(r, c):
        return (r >= 0) & (r < GRID_ROWS) & (c >= 0) & (c < grid_cols)

    lender_ok = [inside(row + dr, col + dc) for dr, dc in OFFSETS]
    borrower_ok = [inside(row - dr, col - dc) for dr, dc in OFFSETS]
    lender = [dom + dr * grid_cols + dc for dr, dc in OFFSETS]
    borrower = [dom - dr * grid_cols - dc for dr, dc in OFFSETS]

    def peer_of(n):
        half = (n + 1) // 2
        off = heads // 2 + half * (1 - 2 * (n % 2))
        return (me + off) % heads

    returned[:, CAP] = jnp.zeros((DIRS, BT, LANES), BF16)

    barrier = pltpu.get_barrier_semaphore()
    near_count = jnp.int32(peers)

    @pl.loop(0, peers)
    def _(n):
        pl.semaphore_signal(barrier, inc=1, device_id={"head": peer_of(n)}, device_id_type=MESH)

    for kk in range(DIRS):
        near_count = near_count + lender_ok[kk].astype(jnp.int32)

        @pl.when(lender_ok[kk])
        def _():
            pl.semaphore_signal(barrier, inc=1, device_id={"dom": lender[kk]}, device_id_type=MESH)

    pairs = ((k_any, k_ref), (v_any, v_ref), (q_any, q_ref), (g_any, g_ref), (bias_any, bias_ref))
    loads = [pltpu.make_async_copy(src, dst, load_sem.at[n]) for n, (src, dst) in enumerate(pairs)]
    for load in loads:
        load.start()

    def pack(part, first, second):
        for i in range(heads // 2):
            cols = slice(i * LANES, (i + 1) * LANES)
            x, y = first[0:MAIN, cols].astype(F32), second[0:MAIN, cols].astype(F32)
            even, odd = merge(x, y)
            main_out[part, 2 * i] = even.astype(BF16)
            main_out[part, 2 * i + 1] = odd.astype(BF16)
            x, y = first[MAIN:, cols].astype(F32), second[MAIN:, cols].astype(F32)
            even, odd = merge(x, y)
            rest_out[part, 2 * i] = even.astype(BF16)
            rest_out[part, 2 * i + 1] = odd.astype(BF16)
        main_in[part, me] = main_out[part, me]
        rest_in[part, me] = rest_out[part, me]

    def to_peer(src, dst, sem, peer):
        return pltpu.make_async_remote_copy(
            src_ref=src, dst_ref=dst, send_sem=in_send.at[sem], recv_sem=in_recv.at[sem],
            device_id={"head": peer}, device_id_type=MESH,
        )

    def send_rows(part, peer):
        to_peer(main_out.at[part, peer], main_in.at[part, me], 2 * part, peer).start()
        to_peer(rest_out.at[part, peer], rest_in.at[part, me], 2 * part + 1, peer).start()

    loads[0].wait()
    loads[1].wait()
    pack(0, k_ref, v_ref)

    pl.semaphore_wait(barrier, near_count)

    @pl.loop(0, peers)
    def _(n):
        send_rows(0, peer_of(n))

    loads[2].wait()
    loads[3].wait()
    pack(1, q_ref, g_ref)

    @pl.loop(0, peers)
    def _(n):
        send_rows(1, peer_of(n))

    window_grads[:, WIN] = jnp.zeros((QB_DOM, BT, LANES), F32)

    def lent_block(kk, c):
        if live_slots(*OFFSETS[kk]) == CAP:
            return send_ref[c, 0, kk]
        return jnp.maximum(jnp.maximum(send_ref[0, 0, kk], send_ref[1, 0, kk]), send_ref[2, 0, kk])

    @pl.loop(0, QB_DOM)
    def _(b):
        names = [near_ref[b, j] for j in range(WIN)]

        def place(first, last):
            at = jnp.int32(WIN)
            for j in range(WIN):
                at = jnp.where((names[j] >= first) & (names[j] <= last), j, at)
            return at

        for e in range(QB_DOM):
            inv_near[b, e] = place(e, e)
        for kk, step in enumerate(OFFSETS):
            live = live_slots(*step)
            for c in range(live):
                e = QB_DOM + kk * CAP + c
                inv_near[b, e] = place(e, e + CAP - live)
        for kk, step in enumerate(OFFSETS):
            at = jnp.int32(CAP)
            for c in range(live_slots(*step)):
                at = jnp.where(borrower_ok[kk] & (lent_block(kk, c) == b), c, at)
            inv_send[b, kk] = at

    for kk in range(DIRS):
        turns[kk] = turn_matrix(orient_ref[0, kk])

    some = pl.ds(0, peers)

    def unpack_rows(part, rows):
        to_peer(main_out.at[part, some], main_in.at[part, some], 2 * part, peer_of(0)).wait_recv()
        to_peer(rest_out.at[part, some], rest_in.at[part, some], 2 * part + 1, peer_of(0)).wait_recv()
        count = MAIN + rest_in.shape[2]
        for source in range(heads):
            base = source * count
            rows[base:base + MAIN] = main_in[part, source].astype(F32)
            rows[base + MAIN:base + count] = rest_in[part, source].astype(F32)

    unpack_rows(0, pair_rows)
    for b in range(QB_DOM):
        ext[b] = pair_rows[b * BT:(b + 1) * BT].astype(BF16)

    def lend(kk):
        live = pl.ds(0, live_slots(*OFFSETS[kk]))
        return pltpu.make_async_remote_copy(
            src_ref=staged.at[kk, live], dst_ref=arrived.at[kk, live],
            send_sem=dom_send.at[kk], recv_sem=dom_recv.at[kk],
            device_id={"dom": borrower[kk]}, device_id_type=MESH,
        )

    for kk, step in enumerate(OFFSETS):
        for c in range(live_slots(*step)):
            staged[kk, c] = ext[lent_block(kk, c)]
    for kk in range(DIRS):

        @pl.when(borrower_ok[kk])
        def _():
            lend(kk).start()

    unpack_rows(1, qg_rows)

    for kk, step in enumerate(OFFSETS):

        @pl.when(lender_ok[kk])
        def _():
            lend(kk).wait_recv()
            for c in range(live_slots(*step)):
                turned = jnp.dot(turns[kk], arrived[kk, c], preferred_element_type=F32).astype(BF16)
                for same in range(c, c + 1 + CAP - live_slots(*step)):
                    ext[QB_DOM + kk * CAP + same] = turned

    loads[4].wait()
    lane = lax.broadcasted_iota(jnp.int32, (1, LANES), 1)
    pair_scale = jnp.where(lane < HD, scale, 1.0).astype(F32)

    for b in range(QB_DOM):
        rows = slice(b * BT, (b + 1) * BT)
        qg = qg_rows[rows]
        mask = left_half(BT)
        qg2 = jnp.concatenate([jnp.where(mask, qg, 0.0), jnp.where(mask, 0.0, qg)], axis=0).astype(BF16)
        window = jnp.concatenate([ext[near_ref[b, j]] for j in range(WIN)], axis=0)
        both = lax.dot_general(qg2, window, (((1,), (1,)), ((), ())), preferred_element_type=F32)
        scores = both[:BT] * scale + bias_ref[0]
        dprobs = both[BT:]
        top = jnp.max(scores, axis=1, keepdims=True)
        exps = jnp.exp(scores - top)
        probs = exps / jnp.sum(exps, axis=1, keepdims=True)
        half = probs.astype(BF16)
        delta = jnp.sum(half.astype(F32) * dprobs, axis=1, keepdims=True)
        dscores = (probs * (dprobs - delta)).astype(BF16)
        gq_rows[rows] = jnp.dot(dscores, window, preferred_element_type=F32) * scale
        stacked = jnp.concatenate([dscores, half], axis=0)
        grads = lax.dot_general(stacked, qg2, (((0,), (0,)), ((), ())), preferred_element_type=F32)
        grads = grads * pair_scale
        for j in range(WIN):
            window_grads[b, j] = grads[j * BT:(j + 1) * BT]

    def slot_grad(e):
        acc = window_grads[0, inv_near[0, e]]
        for b in range(1, QB_DOM):
            acc = acc + window_grads[b, inv_near[b, e]]
        return acc

    def give_back(kk):
        live = pl.ds(0, live_slots(*OFFSETS[kk]))
        return pltpu.make_async_remote_copy(
            src_ref=leaving.at[kk, live], dst_ref=returned.at[kk, live],
            send_sem=back_send.at[kk], recv_sem=back_recv.at[kk],
            device_id={"dom": lender[kk]}, device_id_type=MESH,
        )

    for kk, step in enumerate(OFFSETS):

        @pl.when(lender_ok[kk])
        def _():
            for c in range(live_slots(*step)):
                leaving[kk, c] = lax.dot_general(
                    turns[kk], slot_grad(QB_DOM + kk * CAP + c).astype(BF16),
                    (((0,), (0,)), ((), ())), preferred_element_type=F32,
                ).astype(BF16)

    for kk in range(DIRS):

        @pl.when(lender_ok[kk])
        def _():
            give_back(kk).start()

    def home(src, dst, sem, peer):
        return pltpu.make_async_remote_copy(
            src_ref=src, dst_ref=dst, send_sem=out_send.at[sem], recv_sem=out_recv.at[sem],
            device_id={"head": peer}, device_id_type=MESH,
        )

    count = MAIN + rest_in.shape[2]
    half_main = MAIN // 2
    for peer in range(heads):
        base = peer * count
        first = gq_rows[base:base + half_main]
        second = gq_rows[base + half_main:base + MAIN]
        a_out[peer] = jnp.where(left_half(half_main), first, swap_halves(second)).astype(BF16)

    @pl.loop(0, peers)
    def _(n):
        peer = peer_of(n)
        home(a_out.at[peer], a_in.at[me], 0, peer).start()

    keep = [
        pltpu.make_async_copy(src.at[me], dst.at[me], keep_sem.at[n])
        for n, (src, dst) in enumerate(((a_out, a_in), (b_out, b_in), (c_out, c_in)))
    ]
    keep[0].start()

    for b in range(QB_DOM):
        total_rows[b * BT:(b + 1) * BT] = slot_grad(b)

    for kk in range(DIRS):

        @pl.when(borrower_ok[kk])
        def _():
            give_back(kk).wait_recv()

    for b in range(QB_DOM):
        acc = total_rows[b * BT:(b + 1) * BT]
        for kk in range(DIRS):
            acc = acc + returned[kk, inv_send[b, kk]].astype(F32)
        total_rows[b * BT:(b + 1) * BT] = acc

    for peer in range(heads):
        base = peer * count
        b_out[peer] = total_rows[base:base + MAIN].astype(BF16)
        rest = total_rows[base + MAIN:base + count]
        c_out[peer, 0:2] = rest.astype(BF16)
        rest = gq_rows[base + MAIN:base + count]
        c_out[peer, 2:4] = rest.astype(BF16)

    @pl.loop(0, peers)
    def _(n):
        peer = peer_of(n)
        home(b_out.at[peer], b_in.at[me], 1, peer).start()
        home(c_out.at[peer], c_in.at[me], 2, peer).start()

    keep[1].start()
    keep[2].start()

    home(a_out.at[some], a_in.at[some], 0, peer_of(0)).wait_recv()
    home(b_out.at[some], b_in.at[some], 1, peer_of(0)).wait_recv()
    home(c_out.at[some], c_in.at[some], 2, peer_of(0)).wait_recv()

    for copy in keep:
        copy.wait()

    for part in range(2):
        to_peer(main_out.at[part, some], main_in.at[part, some], 2 * part, peer_of(0)).wait_send()
        to_peer(rest_out.at[part, some], rest_in.at[part, some], 2 * part + 1, peer_of(0)).wait_send()
    for kk in range(DIRS):

        @pl.when(borrower_ok[kk])
        def _():
            lend(kk).wait_send()

        @pl.when(lender_ok[kk])
        def _():
            give_back(kk).wait_send()

    home(a_out.at[some], a_in.at[some], 0, peer_of(0)).wait_send()
    home(b_out.at[some], b_in.at[some], 1, peer_of(0)).wait_send()
    home(c_out.at[some], c_in.at[some], 2, peer_of(0)).wait_send()


def per_device(heads, doms, queries, keys_in, values_in, grad_out, pos_bias, neighbours, send_block, orient):
    rows, width = queries.shape
    rest = rows - MAIN
    tokens = QB_DOM * BT
    whole = pl.BlockSpec(memory_space=pltpu.VMEM)
    anywhere = pl.BlockSpec(memory_space=pl.ANY)
    small = pl.BlockSpec(memory_space=pltpu.SMEM)
    out = jax.ShapeDtypeStruct((rows, width), BF16)
    block = (BT, LANES)
    dma = pltpu.SemaphoreType.DMA
    arrivals = tuple(
        jax.ShapeDtypeStruct((heads, n, LANES), BF16) for n in (MAIN // 2, MAIN, 2 * rest)
    )
    arrived = pl.pallas_call(
        functools.partial(kernel, heads, doms),
        out_shape=arrivals,
        in_specs=[small] * 3 + [anywhere] * 5,
        out_specs=(anywhere,) * 3,
        scratch_shapes=[
            *[pltpu.VMEM((rows, width), BF16)] * 4,
            pltpu.VMEM(pos_bias.shape, F32),
            pltpu.VMEM((2, heads, MAIN, LANES), BF16),
            pltpu.VMEM((2, heads, rest, LANES), BF16),
            pltpu.VMEM((2, heads, MAIN, LANES), BF16),
            pltpu.VMEM((2, heads, rest, LANES), BF16),
            pltpu.VMEM((tokens, LANES), F32),
            pltpu.VMEM((tokens, LANES), F32),
            pltpu.VMEM((SLOTS,) + block, BF16),
            pltpu.VMEM((DIRS, CAP) + block, BF16),
            pltpu.VMEM((DIRS, CAP) + block, BF16),
            pltpu.VMEM((DIRS, BT, BT), BF16),
            pltpu.VMEM((QB_DOM, WIN + 1) + block, F32),
            pltpu.VMEM((tokens, LANES), F32),
            pltpu.VMEM((tokens, LANES), F32),
            pltpu.VMEM((DIRS, CAP) + block, BF16),
            pltpu.VMEM((DIRS, CAP + 1) + block, BF16),
            pltpu.VMEM((heads, MAIN // 2, LANES), BF16),
            pltpu.VMEM((heads, MAIN, LANES), BF16),
            pltpu.VMEM((heads, 2 * rest, LANES), BF16),
            pltpu.SMEM((QB_DOM, SLOTS), jnp.int32),
            pltpu.SMEM((QB_DOM, DIRS), jnp.int32),
            dma((5,)),
            dma((3,)),
            dma((4,)), dma((4,)),
            dma((DIRS,)), dma((DIRS,)),
            dma((DIRS,)), dma((DIRS,)),
            dma((3,)), dma((3,)),
        ],
        compiler_params=pltpu.CompilerParams(collective_id=0, has_side_effects=True),
    )(neighbours, jnp.transpose(send_block, (2, 0, 1)), orient, queries, keys_in, values_in, grad_out, pos_bias)
    return pl.pallas_call(
        lay_out, out_shape=(out, out, out), in_specs=[whole] * 3, out_specs=(whole, whole, whole),
    )(*arrived)


def solution(mesh):
    both = P(("dom", "head"), None)
    return jax.shard_map(
        functools.partial(per_device, mesh.shape["head"], mesh.shape["dom"]),
        mesh=mesh,
        in_specs=(both, both, both, both, P("head", None, None), P("dom", None), P("dom", None, None), P("dom", None)),
        out_specs=(both, both, both),
        check_vma=False,
    )
```

```python
import functools

import jax
import jax.numpy as jnp
from jax import lax
from jax.experimental import pallas as pl
from jax.experimental.pallas import tpu as pltpu
from jax.sharding import PartitionSpec as P

HD = 64
LANES = 128
PATCH = 8
BT = 64
GRID_ROWS = 4
DIRS = 8
WIN = 9
QB_DOM = 9
CAP = 3
MAIN = 16
SLOTS = QB_DOM + DIRS * CAP
OFFSETS = [(-1, -1), (-1, 0), (-1, 1), (0, -1), (0, 1), (1, -1), (1, 0), (1, 1)]
MESH = pl.DeviceIdType.MESH
STAGES = [(0, 9), (9, 17), (17, 23), (23, 31)]
STAGE_BLOCKS = [(0,), (1, 8), (2, 7), (3, 6, 4, 5)]
F32 = jnp.float32
BF16 = jnp.bfloat16


def live_slots(row_step, col_step):
    return 1 if row_step and col_step else CAP


def turn_matrix(orient_id):
    token = lax.broadcasted_iota(jnp.int32, (BT, BT), 0)
    target = lax.broadcasted_iota(jnp.int32, (BT, BT), 1)
    r = lax.shift_right_logical(token, 3)
    s = lax.bitwise_and(token, 7)
    flip_r = lax.bitwise_and(orient_id, 1)
    flip_s = lax.bitwise_and(lax.shift_right_logical(orient_id, 1), 1)
    swap = lax.bitwise_and(lax.shift_right_logical(orient_id, 2), 1)
    r2 = r + flip_r * (PATCH - 1 - 2 * r)
    s2 = s + flip_s * (PATCH - 1 - 2 * s)
    mapped = swap * (PATCH * s2 + r2) + (1 - swap) * (PATCH * r2 + s2)
    return jnp.where(target == mapped, 1.0, 0.0).astype(BF16)


def left_half(rows):
    return lax.broadcasted_iota(jnp.int32, (rows, LANES), 1) < HD


def swap_halves(x):
    return pltpu.roll(x, HD, 1)


def merge(x, y):
    mask = left_half(x.shape[0])
    return jnp.where(mask, x, swap_halves(y)), jnp.where(mask, swap_halves(x), y)


def lay_out(a_ref, b_ref, c_ref, gq_ref, gk_ref, gv_ref):
    heads, half_main = a_ref.shape[:2]
    rest = c_ref.shape[1] // 2
    for i in range(heads // 2):
        cols = slice(i * LANES, (i + 1) * LANES)
        first, second = merge(a_ref[2 * i].astype(F32), a_ref[2 * i + 1].astype(F32))
        gq_ref[0:half_main, cols] = first.astype(BF16)
        gq_ref[half_main:MAIN, cols] = second.astype(BF16)
        first, second = merge(b_ref[2 * i].astype(F32), b_ref[2 * i + 1].astype(F32))
        gk_ref[0:MAIN, cols] = first.astype(BF16)
        gv_ref[0:MAIN, cols] = second.astype(BF16)
        first, second = merge(c_ref[2 * i].astype(F32), c_ref[2 * i + 1].astype(F32))
        gk_ref[MAIN:, cols] = first[0:rest].astype(BF16)
        gq_ref[MAIN:, cols] = first[rest:].astype(BF16)
        gv_ref[MAIN:, cols] = second[0:rest].astype(BF16)


def kernel(
    heads, doms,
    near_ref, send_ref, orient_ref, q_any, k_any, v_any, g_any, bias_any,
    a_in, b_in, c_in,
    q_ref, k_ref, v_ref, g_ref, bias_ref,
    main_out, rest_out, main_in, rest_in,
    pair_rows, qg_rows, ext, staged, arrived, turns,
    window_grads, gq_rows, total_rows, leaving, returned,
    a_out, b_out, c_out,
    inv_near, inv_send,
    load_sem, keep_sem,
    in_send, in_recv, dom_send, dom_recv, back_send, back_recv, out_send, out_recv,
):
    grid_cols = doms // GRID_ROWS
    peers = heads - 1
    me = lax.axis_index("head")
    dom = lax.axis_index("dom")
    row = dom // grid_cols
    col = dom % grid_cols
    scale = HD ** (-0.5)

    def inside(r, c):
        return (r >= 0) & (r < GRID_ROWS) & (c >= 0) & (c < grid_cols)

    lender_ok = [inside(row + dr, col + dc) for dr, dc in OFFSETS]
    borrower_ok = [inside(row - dr, col - dc) for dr, dc in OFFSETS]
    lender = [dom + dr * grid_cols + dc for dr, dc in OFFSETS]
    borrower = [dom - dr * grid_cols - dc for dr, dc in OFFSETS]

    def peer_of(n):
        half = (n + 1) // 2
        off = heads // 2 + half * (1 - 2 * (n % 2))
        return (me + off) % heads

    returned[:, CAP] = jnp.zeros((DIRS, BT, LANES), BF16)

    barrier = pltpu.get_barrier_semaphore()
    near_count = jnp.int32(peers)

    @pl.loop(0, peers)
    def _(n):
        pl.semaphore_signal(barrier, inc=1, device_id={"head": peer_of(n)}, device_id_type=MESH)

    for kk in range(DIRS):
        near_count = near_count + lender_ok[kk].astype(jnp.int32)

        @pl.when(lender_ok[kk])
        def _():
            pl.semaphore_signal(barrier, inc=1, device_id={"dom": lender[kk]}, device_id_type=MESH)

    pairs = ((k_any, k_ref), (v_any, v_ref), (q_any, q_ref), (g_any, g_ref), (bias_any, bias_ref))
    loads = [pltpu.make_async_copy(src, dst, load_sem.at[n]) for n, (src, dst) in enumerate(pairs)]
    for load in loads:
        load.start()

    def pack(part, first, second):
        for i in range(heads // 2):
            cols = slice(i * LANES, (i + 1) * LANES)
            x, y = first[0:MAIN, cols].astype(F32), second[0:MAIN, cols].astype(F32)
            even, odd = merge(x, y)
            main_out[part, 2 * i] = even.astype(BF16)
            main_out[part, 2 * i + 1] = odd.astype(BF16)
            x, y = first[MAIN:, cols].astype(F32), second[MAIN:, cols].astype(F32)
            even, odd = merge(x, y)
            rest_out[part, 2 * i] = even.astype(BF16)
            rest_out[part, 2 * i + 1] = odd.astype(BF16)
        main_in[part, me] = main_out[part, me]
        rest_in[part, me] = rest_out[part, me]

    def to_peer(src, dst, sem, peer, stage=0):
        return pltpu.make_async_remote_copy(
            src_ref=src, dst_ref=dst, send_sem=in_send.at[sem], recv_sem=in_recv.at[sem, stage],
            device_id={"head": peer}, device_id_type=MESH,
        )

    def send_rows(part, peer, stage=0):
        to_peer(main_out.at[part, peer], main_in.at[part, me], 2 * part, peer, stage).start()
        to_peer(rest_out.at[part, peer], rest_in.at[part, me], 2 * part + 1, peer, stage).start()

    loads[0].wait()
    loads[1].wait()
    pack(0, k_ref, v_ref)

    pl.semaphore_wait(barrier, near_count)

    @pl.loop(0, peers)
    def _(n):
        send_rows(0, peer_of(n))

    loads[2].wait()
    loads[3].wait()
    pack(1, q_ref, g_ref)

    for stage, (first, last) in enumerate(STAGES):

        @pl.loop(first, last)
        def _(n):
            send_rows(1, peer_of(n), stage)

    window_grads[:, WIN] = jnp.zeros((QB_DOM, BT, LANES), F32)

    def lent_block(kk, c):
        if live_slots(*OFFSETS[kk]) == CAP:
            return send_ref[c, 0, kk]
        return jnp.maximum(jnp.maximum(send_ref[0, 0, kk], send_ref[1, 0, kk]), send_ref[2, 0, kk])

    @pl.loop(0, QB_DOM)
    def _(b):
        names = [near_ref[b, j] for j in range(WIN)]

        def place(first, last):
            at = jnp.int32(WIN)
            for j in range(WIN):
                at = jnp.where((names[j] >= first) & (names[j] <= last), j, at)
            return at

        for e in range(QB_DOM):
            inv_near[b, e] = place(e, e)
        for kk, step in enumerate(OFFSETS):
            live = live_slots(*step)
            for c in range(live):
                e = QB_DOM + kk * CAP + c
                inv_near[b, e] = place(e, e + CAP - live)
        for kk, step in enumerate(OFFSETS):
            at = jnp.int32(CAP)
            for c in range(live_slots(*step)):
                at = jnp.where(borrower_ok[kk] & (lent_block(kk, c) == b), c, at)
            inv_send[b, kk] = at

    for kk in range(DIRS):
        turns[kk] = turn_matrix(orient_ref[0, kk])

    some = pl.ds(0, peers)

    def unpack_rows(part, rows):
        to_peer(main_out.at[part, some], main_in.at[part, some], 2 * part, peer_of(0)).wait_recv()
        to_peer(rest_out.at[part, some], rest_in.at[part, some], 2 * part + 1, peer_of(0)).wait_recv()
        count = MAIN + rest_in.shape[2]
        for source in range(heads):
            base = source * count
            rows[base:base + MAIN] = main_in[part, source].astype(F32)
            rows[base + MAIN:base + count] = rest_in[part, source].astype(F32)

    unpack_rows(0, pair_rows)
    for b in range(QB_DOM):
        ext[b] = pair_rows[b * BT:(b + 1) * BT].astype(BF16)

    def lend(kk):
        live = pl.ds(0, live_slots(*OFFSETS[kk]))
        return pltpu.make_async_remote_copy(
            src_ref=staged.at[kk, live], dst_ref=arrived.at[kk, live],
            send_sem=dom_send.at[kk], recv_sem=dom_recv.at[kk],
            device_id={"dom": borrower[kk]}, device_id_type=MESH,
        )

    for kk, step in enumerate(OFFSETS):
        for c in range(live_slots(*step)):
            staged[kk, c] = ext[lent_block(kk, c)]
    for kk in range(DIRS):

        @pl.when(borrower_ok[kk])
        def _():
            lend(kk).start()

    count = MAIN + rest_in.shape[2]

    def place_rows(source):
        base = source * count
        qg_rows[pl.ds(base, MAIN)] = main_in[1, source].astype(F32)
        qg_rows[pl.ds(base + MAIN, count - MAIN)] = rest_in[1, source].astype(F32)

    def stage_rows(stage):
        first, last = STAGES[stage]
        part = pl.ds(0, last - first)
        to_peer(main_out.at[1, part], main_in.at[1, part], 2, peer_of(0), stage).wait_recv()
        to_peer(rest_out.at[1, part], rest_in.at[1, part], 3, peer_of(0), stage).wait_recv()
        for n in range(first, last):
            place_rows(peer_of(n))

    place_rows(me)

    for kk, step in enumerate(OFFSETS):

        @pl.when(lender_ok[kk])
        def _():
            lend(kk).wait_recv()
            for c in range(live_slots(*step)):
                turned = jnp.dot(turns[kk], arrived[kk, c], preferred_element_type=F32).astype(BF16)
                for same in range(c, c + 1 + CAP - live_slots(*step)):
                    ext[QB_DOM + kk * CAP + same] = turned

    loads[4].wait()
    lane = lax.broadcasted_iota(jnp.int32, (1, LANES), 1)
    pair_scale = jnp.where(lane < HD, scale, 1.0).astype(F32)

    far_block = (((me + heads // 2) % heads) * count + count // 2) // BT

    def attend(b):
        rows = pl.ds(pl.multiple_of(b * BT, BT), BT)
        qg = qg_rows[rows]
        mask = left_half(BT)
        qg2 = jnp.concatenate([jnp.where(mask, qg, 0.0), jnp.where(mask, 0.0, qg)], axis=0).astype(BF16)
        window = jnp.concatenate([ext[near_ref[b, j]] for j in range(WIN)], axis=0)
        both = lax.dot_general(qg2, window, (((1,), (1,)), ((), ())), preferred_element_type=F32)
        scores = both[:BT] * scale + bias_ref[0]
        dprobs = both[BT:]
        top = jnp.max(scores, axis=1, keepdims=True)
        exps = jnp.exp(scores - top)
        probs = exps / jnp.sum(exps, axis=1, keepdims=True)
        half = probs.astype(BF16)
        delta = jnp.sum(half.astype(F32) * dprobs, axis=1, keepdims=True)
        dscores = (probs * (dprobs - delta)).astype(BF16)
        gq_rows[rows] = jnp.dot(dscores, window, preferred_element_type=F32) * scale
        stacked = jnp.concatenate([dscores, half], axis=0)
        grads = lax.dot_general(stacked, qg2, (((0,), (0,)), ((), ())), preferred_element_type=F32)
        grads = grads * pair_scale
        for j in range(WIN):
            window_grads[b, j] = grads[j * BT:(j + 1) * BT]

    for stage, blocks in enumerate(STAGE_BLOCKS):
        stage_rows(stage)
        for block in blocks:
            attend((far_block + block) % QB_DOM)

    def slot_grad(e):
        acc = window_grads[0, inv_near[0, e]]
        for b in range(1, QB_DOM):
            acc = acc + window_grads[b, inv_near[b, e]]
        return acc

    def give_back(kk):
        live = pl.ds(0, live_slots(*OFFSETS[kk]))
        return pltpu.make_async_remote_copy(
            src_ref=leaving.at[kk, live], dst_ref=returned.at[kk, live],
            send_sem=back_send.at[kk], recv_sem=back_recv.at[kk],
            device_id={"dom": lender[kk]}, device_id_type=MESH,
        )

    for kk, step in enumerate(OFFSETS):

        @pl.when(lender_ok[kk])
        def _():
            for c in range(live_slots(*step)):
                leaving[kk, c] = lax.dot_general(
                    turns[kk], slot_grad(QB_DOM + kk * CAP + c).astype(BF16),
                    (((0,), (0,)), ((), ())), preferred_element_type=F32,
                ).astype(BF16)

    for kk in range(DIRS):

        @pl.when(lender_ok[kk])
        def _():
            give_back(kk).start()

    def home(src, dst, sem, peer):
        return pltpu.make_async_remote_copy(
            src_ref=src, dst_ref=dst, send_sem=out_send.at[sem], recv_sem=out_recv.at[sem],
            device_id={"head": peer}, device_id_type=MESH,
        )

    half_main = MAIN // 2
    for peer in range(heads):
        base = peer * count
        first = gq_rows[base:base + half_main]
        second = gq_rows[base + half_main:base + MAIN]
        a_out[peer] = jnp.where(left_half(half_main), first, swap_halves(second)).astype(BF16)

    @pl.loop(0, peers)
    def _(n):
        peer = peer_of(n)
        home(a_out.at[peer], a_in.at[me], 0, peer).start()

    keep = [
        pltpu.make_async_copy(src.at[me], dst.at[me], keep_sem.at[n])
        for n, (src, dst) in enumerate(((a_out, a_in), (b_out, b_in), (c_out, c_in)))
    ]
    keep[0].start()

    for b in range(QB_DOM):
        total_rows[b * BT:(b + 1) * BT] = slot_grad(b)

    for kk in range(DIRS):

        @pl.when(borrower_ok[kk])
        def _():
            give_back(kk).wait_recv()

    for b in range(QB_DOM):
        acc = total_rows[b * BT:(b + 1) * BT]
        for kk in range(DIRS):
            acc = acc + returned[kk, inv_send[b, kk]].astype(F32)
        total_rows[b * BT:(b + 1) * BT] = acc

    for peer in range(heads):
        base = peer * count
        b_out[peer] = total_rows[base:base + MAIN].astype(BF16)
        rest = total_rows[base + MAIN:base + count]
        c_out[peer, 0:2] = rest.astype(BF16)
        rest = gq_rows[base + MAIN:base + count]
        c_out[peer, 2:4] = rest.astype(BF16)

    @pl.loop(0, peers)
    def _(n):
        peer = peer_of(n)
        home(b_out.at[peer], b_in.at[me], 1, peer).start()
        home(c_out.at[peer], c_in.at[me], 2, peer).start()

    keep[1].start()
    keep[2].start()

    home(a_out.at[some], a_in.at[some], 0, peer_of(0)).wait_recv()
    home(b_out.at[some], b_in.at[some], 1, peer_of(0)).wait_recv()
    home(c_out.at[some], c_in.at[some], 2, peer_of(0)).wait_recv()

    for copy in keep:
        copy.wait()

    for part in range(2):
        to_peer(main_out.at[part, some], main_in.at[part, some], 2 * part, peer_of(0)).wait_send()
        to_peer(rest_out.at[part, some], rest_in.at[part, some], 2 * part + 1, peer_of(0)).wait_send()
    for kk in range(DIRS):

        @pl.when(borrower_ok[kk])
        def _():
            lend(kk).wait_send()

        @pl.when(lender_ok[kk])
        def _():
            give_back(kk).wait_send()

    home(a_out.at[some], a_in.at[some], 0, peer_of(0)).wait_send()
    home(b_out.at[some], b_in.at[some], 1, peer_of(0)).wait_send()
    home(c_out.at[some], c_in.at[some], 2, peer_of(0)).wait_send()


def per_device(heads, doms, queries, keys_in, values_in, grad_out, pos_bias, neighbours, send_block, orient):
    rows, width = queries.shape
    rest = rows - MAIN
    tokens = QB_DOM * BT
    whole = pl.BlockSpec(memory_space=pltpu.VMEM)
    anywhere = pl.BlockSpec(memory_space=pl.ANY)
    small = pl.BlockSpec(memory_space=pltpu.SMEM)
    out = jax.ShapeDtypeStruct((rows, width), BF16)
    block = (BT, LANES)
    dma = pltpu.SemaphoreType.DMA
    arrivals = tuple(
        jax.ShapeDtypeStruct((heads, n, LANES), BF16) for n in (MAIN // 2, MAIN, 2 * rest)
    )
    arrived = pl.pallas_call(
        functools.partial(kernel, heads, doms),
        out_shape=arrivals,
        in_specs=[small] * 3 + [anywhere] * 5,
        out_specs=(anywhere,) * 3,
        scratch_shapes=[
            *[pltpu.VMEM((rows, width), BF16)] * 4,
            pltpu.VMEM(pos_bias.shape, F32),
            pltpu.VMEM((2, heads, MAIN, LANES), BF16),
            pltpu.VMEM((2, heads, rest, LANES), BF16),
            pltpu.VMEM((2, heads, MAIN, LANES), BF16),
            pltpu.VMEM((2, heads, rest, LANES), BF16),
            pltpu.VMEM((tokens, LANES), F32),
            pltpu.VMEM((tokens, LANES), F32),
            pltpu.VMEM((SLOTS,) + block, BF16),
            pltpu.VMEM((DIRS, CAP) + block, BF16),
            pltpu.VMEM((DIRS, CAP) + block, BF16),
            pltpu.VMEM((DIRS, BT, BT), BF16),
            pltpu.VMEM((QB_DOM, WIN + 1) + block, F32),
            pltpu.VMEM((tokens, LANES), F32),
            pltpu.VMEM((tokens, LANES), F32),
            pltpu.VMEM((DIRS, CAP) + block, BF16),
            pltpu.VMEM((DIRS, CAP + 1) + block, BF16),
            pltpu.VMEM((heads, MAIN // 2, LANES), BF16),
            pltpu.VMEM((heads, MAIN, LANES), BF16),
            pltpu.VMEM((heads, 2 * rest, LANES), BF16),
            pltpu.SMEM((QB_DOM, SLOTS), jnp.int32),
            pltpu.SMEM((QB_DOM, DIRS), jnp.int32),
            dma((5,)),
            dma((3,)),
            dma((4,)), dma((4, len(STAGES))),
            dma((DIRS,)), dma((DIRS,)),
            dma((DIRS,)), dma((DIRS,)),
            dma((3,)), dma((3,)),
        ],
        compiler_params=pltpu.CompilerParams(collective_id=0, has_side_effects=True),
    )(neighbours, jnp.transpose(send_block, (2, 0, 1)), orient, queries, keys_in, values_in, grad_out, pos_bias)
    return pl.pallas_call(
        lay_out, out_shape=(out, out, out), in_specs=[whole] * 3, out_specs=(whole, whole, whole),
    )(*arrived)


def solution(mesh):
    both = P(("dom", "head"), None)
    return jax.shard_map(
        functools.partial(per_device, mesh.shape["head"], mesh.shape["dom"]),
        mesh=mesh,
        in_specs=(both, both, both, both, P("head", None, None), P("dom", None), P("dom", None, None), P("dom", None)),
        out_specs=(both, both, both),
        check_vma=False,
    )
```

```python
import functools

import jax
import jax.numpy as jnp
from jax import lax
from jax.experimental import pallas as pl
from jax.experimental.pallas import tpu as pltpu
from jax.sharding import PartitionSpec as P

HD = 64
LANES = 128
PATCH = 8
BT = 64
GRID_ROWS = 4
DIRS = 8
WIN = 9
QB_DOM = 9
CAP = 3
MAIN = 16
SLOTS = QB_DOM + DIRS * CAP
OFFSETS = [(-1, -1), (-1, 0), (-1, 1), (0, -1), (0, 1), (1, -1), (1, 0), (1, 1)]
MESH = pl.DeviceIdType.MESH
STAGES = [(23, 31), (15, 23), (9, 15), (0, 9)]
STAGE_BLOCKS = [(0,), (1, 8), (2, 7), (3, 6, 4, 5)]
F32 = jnp.float32
BF16 = jnp.bfloat16


def live_slots(row_step, col_step):
    return 1 if row_step and col_step else CAP


def turn_matrix(orient_id):
    token = lax.broadcasted_iota(jnp.int32, (BT, BT), 0)
    target = lax.broadcasted_iota(jnp.int32, (BT, BT), 1)
    r = lax.shift_right_logical(token, 3)
    s = lax.bitwise_and(token, 7)
    flip_r = lax.bitwise_and(orient_id, 1)
    flip_s = lax.bitwise_and(lax.shift_right_logical(orient_id, 1), 1)
    swap = lax.bitwise_and(lax.shift_right_logical(orient_id, 2), 1)
    r2 = r + flip_r * (PATCH - 1 - 2 * r)
    s2 = s + flip_s * (PATCH - 1 - 2 * s)
    mapped = swap * (PATCH * s2 + r2) + (1 - swap) * (PATCH * r2 + s2)
    return jnp.where(target == mapped, 1.0, 0.0).astype(BF16)


def left_half(rows):
    return lax.broadcasted_iota(jnp.int32, (rows, LANES), 1) < HD


def swap_halves(x):
    return pltpu.roll(x, HD, 1)


def merge(x, y):
    mask = left_half(x.shape[0])
    return jnp.where(mask, x, swap_halves(y)), jnp.where(mask, swap_halves(x), y)


def lay_out(a_ref, b_ref, c_ref, d_ref, gq_ref, gk_ref, gv_ref):
    heads, half_main = a_ref.shape[:2]
    for i in range(heads // 2):
        cols = slice(i * LANES, (i + 1) * LANES)
        first, second = merge(a_ref[2 * i].astype(F32), a_ref[2 * i + 1].astype(F32))
        gq_ref[0:half_main, cols] = first.astype(BF16)
        gq_ref[half_main:MAIN, cols] = second.astype(BF16)
        first, second = merge(b_ref[2 * i].astype(F32), b_ref[2 * i + 1].astype(F32))
        gk_ref[0:MAIN, cols] = first.astype(BF16)
        gv_ref[0:MAIN, cols] = second.astype(BF16)
        first, second = merge(c_ref[2 * i].astype(F32), c_ref[2 * i + 1].astype(F32))
        gk_ref[MAIN:, cols] = first.astype(BF16)
        gv_ref[MAIN:, cols] = second.astype(BF16)
        first, _ = merge(d_ref[2 * i].astype(F32), d_ref[2 * i + 1].astype(F32))
        gq_ref[MAIN:, cols] = first.astype(BF16)


def kernel(
    heads, doms,
    near_any, send_any, orient_any, q_any, k_any, v_any, g_any, bias_any,
    a_in, b_in, c_in, d_in,
    q_ref, k_ref, v_ref, g_ref, bias_ref,
    main_out, rest_out, main_in, rest_in,
    pair_rows, qg_rows, ext, staged, arrived, turns,
    window_grads, gq_rows, total_rows, leaving, returned,
    a_out, b_out, c_out, d_out,
    near_ref, send_ref, orient_ref,
    inv_near, inv_send,
    load_sem, keep_sem,
    in_send, in_recv, dom_send, dom_recv, back_send, back_recv, out_send, out_recv,
):
    grid_cols = doms // GRID_ROWS
    peers = heads - 1
    me = lax.axis_index("head")
    dom = lax.axis_index("dom")
    row = dom // grid_cols
    col = dom % grid_cols
    scale = HD ** (-0.5)

    def inside(r, c):
        return (r >= 0) & (r < GRID_ROWS) & (c >= 0) & (c < grid_cols)

    lender_ok = [inside(row + dr, col + dc) for dr, dc in OFFSETS]
    borrower_ok = [inside(row - dr, col - dc) for dr, dc in OFFSETS]
    lender = [dom + dr * grid_cols + dc for dr, dc in OFFSETS]
    borrower = [dom - dr * grid_cols - dc for dr, dc in OFFSETS]

    def peer_of(n):
        half = (n + 1) // 2
        off = heads // 2 + half * (1 - 2 * (n % 2))
        return (me + off) % heads

    returned[:, CAP] = jnp.zeros((DIRS, BT, LANES), BF16)

    barrier = pltpu.get_barrier_semaphore()
    near_count = jnp.int32(peers)

    @pl.loop(0, peers)
    def _(n):
        pl.semaphore_signal(barrier, inc=1, device_id={"head": peer_of(n)}, device_id_type=MESH)

    for kk in range(DIRS):
        near_count = near_count + lender_ok[kk].astype(jnp.int32)

        @pl.when(lender_ok[kk])
        def _():
            pl.semaphore_signal(barrier, inc=1, device_id={"dom": lender[kk]}, device_id_type=MESH)

    pairs = ((k_any, k_ref), (v_any, v_ref), (q_any, q_ref), (g_any, g_ref), (bias_any, bias_ref),
             (near_any, near_ref), (send_any, send_ref), (orient_any, orient_ref))
    loads = [pltpu.make_async_copy(src, dst, load_sem.at[n]) for n, (src, dst) in enumerate(pairs)]
    for load in loads:
        load.start()

    def pack(part, first, second):
        for i in range(heads // 2):
            cols = slice(i * LANES, (i + 1) * LANES)
            x, y = first[0:MAIN, cols].astype(F32), second[0:MAIN, cols].astype(F32)
            even, odd = merge(x, y)
            main_out[part, 2 * i] = even.astype(BF16)
            main_out[part, 2 * i + 1] = odd.astype(BF16)
            x, y = first[MAIN:, cols].astype(F32), second[MAIN:, cols].astype(F32)
            even, odd = merge(x, y)
            rest_out[part, 2 * i] = even.astype(BF16)
            rest_out[part, 2 * i + 1] = odd.astype(BF16)
        main_in[part, me] = main_out[part, me]
        rest_in[part, me] = rest_out[part, me]

    def to_peer(src, dst, sem, peer, stage=0):
        return pltpu.make_async_remote_copy(
            src_ref=src, dst_ref=dst, send_sem=in_send.at[sem], recv_sem=in_recv.at[sem, stage],
            device_id={"head": peer}, device_id_type=MESH,
        )

    def send_rows(part, peer, stage=0):
        to_peer(main_out.at[part, peer], main_in.at[part, me], 2 * part, peer, stage).start()
        to_peer(rest_out.at[part, peer], rest_in.at[part, me], 2 * part + 1, peer, stage).start()

    loads[0].wait()
    loads[1].wait()
    pack(0, k_ref, v_ref)

    pl.semaphore_wait(barrier, near_count)

    @pl.loop(0, peers)
    def _(n):
        send_rows(0, peer_of(n))

    loads[2].wait()
    loads[3].wait()
    pack(1, q_ref, g_ref)

    for stage, (first, last) in reversed(list(enumerate(STAGES))):

        @pl.loop(first, last)
        def _(n):
            send_rows(1, peer_of(n), stage)

    window_grads[:, WIN] = jnp.zeros((QB_DOM, BT, LANES), F32)

    for load in loads[5:]:
        load.wait()

    def lent_block(kk, c):
        if live_slots(*OFFSETS[kk]) == CAP:
            return send_ref[c, 0, kk]
        return jnp.maximum(jnp.maximum(send_ref[0, 0, kk], send_ref[1, 0, kk]), send_ref[2, 0, kk])

    @pl.loop(0, QB_DOM)
    def _(b):
        names = [near_ref[b, j] for j in range(WIN)]

        def place(first, last):
            at = jnp.int32(WIN)
            for j in range(WIN):
                at = jnp.where((names[j] >= first) & (names[j] <= last), j, at)
            return at

        for e in range(QB_DOM):
            inv_near[b, e] = place(e, e)
        for kk, step in enumerate(OFFSETS):
            live = live_slots(*step)
            for c in range(live):
                e = QB_DOM + kk * CAP + c
                inv_near[b, e] = place(e, e + CAP - live)
        for kk, step in enumerate(OFFSETS):
            at = jnp.int32(CAP)
            for c in range(live_slots(*step)):
                at = jnp.where(borrower_ok[kk] & (lent_block(kk, c) == b), c, at)
            inv_send[b, kk] = at

    for kk in range(DIRS):
        turns[kk] = turn_matrix(orient_ref[0, kk])

    some = pl.ds(0, peers)

    def unpack_rows(part, rows):
        to_peer(main_out.at[part, some], main_in.at[part, some], 2 * part, peer_of(0)).wait_recv()
        to_peer(rest_out.at[part, some], rest_in.at[part, some], 2 * part + 1, peer_of(0)).wait_recv()
        count = MAIN + rest_in.shape[2]
        for source in range(heads):
            base = source * count
            rows[base:base + MAIN] = main_in[part, source].astype(F32)
            rows[base + MAIN:base + count] = rest_in[part, source].astype(F32)

    unpack_rows(0, pair_rows)
    for b in range(QB_DOM):
        ext[b] = pair_rows[b * BT:(b + 1) * BT].astype(BF16)

    def lend(kk):
        live = pl.ds(0, live_slots(*OFFSETS[kk]))
        return pltpu.make_async_remote_copy(
            src_ref=staged.at[kk, live], dst_ref=arrived.at[kk, live],
            send_sem=dom_send.at[kk], recv_sem=dom_recv.at[kk],
            device_id={"dom": borrower[kk]}, device_id_type=MESH,
        )

    for kk, step in enumerate(OFFSETS):
        for c in range(live_slots(*step)):
            staged[kk, c] = ext[lent_block(kk, c)]
    for kk in range(DIRS):

        @pl.when(borrower_ok[kk])
        def _():
            lend(kk).start()

    count = MAIN + rest_in.shape[2]

    def place_rows(source):
        base = source * count
        qg_rows[pl.ds(base, MAIN)] = main_in[1, source].astype(F32)
        qg_rows[pl.ds(base + MAIN, count - MAIN)] = rest_in[1, source].astype(F32)

    def stage_rows(stage):
        first, last = STAGES[stage]
        part = pl.ds(0, last - first)
        to_peer(main_out.at[1, part], main_in.at[1, part], 2, peer_of(0), stage).wait_recv()
        to_peer(rest_out.at[1, part], rest_in.at[1, part], 3, peer_of(0), stage).wait_recv()
        for n in range(first, last):
            place_rows(peer_of(n))

    place_rows(me)

    for kk, step in enumerate(OFFSETS):

        @pl.when(lender_ok[kk])
        def _():
            lend(kk).wait_recv()
            for c in range(live_slots(*step)):
                turned = jnp.dot(turns[kk], arrived[kk, c], preferred_element_type=F32).astype(BF16)
                for same in range(c, c + 1 + CAP - live_slots(*step)):
                    ext[QB_DOM + kk * CAP + same] = turned

    loads[4].wait()
    lane = lax.broadcasted_iota(jnp.int32, (1, LANES), 1)
    pair_scale = jnp.where(lane < HD, scale, 1.0).astype(F32)

    far_block = (me * count + count // 2) // BT

    def attend(b):
        rows = pl.ds(pl.multiple_of(b * BT, BT), BT)
        qg = qg_rows[rows]
        mask = left_half(BT)
        qg2 = jnp.concatenate([jnp.where(mask, qg, 0.0), jnp.where(mask, 0.0, qg)], axis=0).astype(BF16)
        window = jnp.concatenate([ext[near_ref[b, j]] for j in range(WIN)], axis=0)
        both = lax.dot_general(qg2, window, (((1,), (1,)), ((), ())), preferred_element_type=F32)
        scores = both[:BT] * scale + bias_ref[0]
        dprobs = both[BT:]
        top = jnp.max(scores, axis=1, keepdims=True)
        exps = jnp.exp(scores - top)
        probs = exps / jnp.sum(exps, axis=1, keepdims=True)
        half = probs.astype(BF16)
        delta = jnp.sum(half.astype(F32) * dprobs, axis=1, keepdims=True)
        dscores = (probs * (dprobs - delta)).astype(BF16)
        gq_rows[rows] = jnp.dot(dscores, window, preferred_element_type=F32) * scale
        stacked = jnp.concatenate([dscores, half], axis=0)
        grads = lax.dot_general(stacked, qg2, (((0,), (0,)), ((), ())), preferred_element_type=F32)
        grads = grads * pair_scale
        for j in range(WIN):
            window_grads[b, j] = grads[j * BT:(j + 1) * BT]

    for stage, blocks in enumerate(STAGE_BLOCKS):
        stage_rows(stage)
        for block in blocks:
            attend((far_block + block) % QB_DOM)

    def slot_grad(e):
        acc = window_grads[0, inv_near[0, e]]
        for b in range(1, QB_DOM):
            acc = acc + window_grads[b, inv_near[b, e]]
        return acc

    def give_back(kk):
        live = pl.ds(0, live_slots(*OFFSETS[kk]))
        return pltpu.make_async_remote_copy(
            src_ref=leaving.at[kk, live], dst_ref=returned.at[kk, live],
            send_sem=back_send.at[kk], recv_sem=back_recv.at[kk],
            device_id={"dom": lender[kk]}, device_id_type=MESH,
        )

    for kk, step in enumerate(OFFSETS):

        @pl.when(lender_ok[kk])
        def _():
            for c in range(live_slots(*step)):
                leaving[kk, c] = lax.dot_general(
                    turns[kk], slot_grad(QB_DOM + kk * CAP + c).astype(BF16),
                    (((0,), (0,)), ((), ())), preferred_element_type=F32,
                ).astype(BF16)

    for kk in range(DIRS):

        @pl.when(lender_ok[kk])
        def _():
            give_back(kk).start()

    def home(src, dst, sem, peer):
        return pltpu.make_async_remote_copy(
            src_ref=src, dst_ref=dst, send_sem=out_send.at[sem], recv_sem=out_recv.at[sem],
            device_id={"head": peer}, device_id_type=MESH,
        )

    half_main = MAIN // 2
    for peer in range(heads):
        base = peer * count
        first = gq_rows[base:base + half_main]
        second = gq_rows[base + half_main:base + MAIN]
        a_out[peer] = jnp.where(left_half(half_main), first, swap_halves(second)).astype(BF16)
        d_out[peer] = gq_rows[base + MAIN:base + count].astype(BF16)

    @pl.loop(0, peers)
    def _(n):
        peer = peer_of(n)
        home(a_out.at[peer], a_in.at[me], 0, peer).start()
        home(d_out.at[peer], d_in.at[me], 3, peer).start()

    keep = [
        pltpu.make_async_copy(src.at[me], dst.at[me], keep_sem.at[n])
        for n, (src, dst) in enumerate(((a_out, a_in), (b_out, b_in), (c_out, c_in), (d_out, d_in)))
    ]
    keep[0].start()
    keep[3].start()

    for b in range(QB_DOM):
        total_rows[b * BT:(b + 1) * BT] = slot_grad(b)

    for kk in range(DIRS):

        @pl.when(borrower_ok[kk])
        def _():
            give_back(kk).wait_recv()

    for b in range(QB_DOM):
        acc = total_rows[b * BT:(b + 1) * BT]
        for kk in range(DIRS):
            acc = acc + returned[kk, inv_send[b, kk]].astype(F32)
        total_rows[b * BT:(b + 1) * BT] = acc

    for peer in range(heads):
        base = peer * count
        b_out[peer] = total_rows[base:base + MAIN].astype(BF16)
        c_out[peer] = total_rows[base + MAIN:base + count].astype(BF16)

    @pl.loop(0, peers)
    def _(n):
        peer = peer_of(n)
        home(b_out.at[peer], b_in.at[me], 1, peer).start()
        home(c_out.at[peer], c_in.at[me], 2, peer).start()

    keep[1].start()
    keep[2].start()

    home(a_out.at[some], a_in.at[some], 0, peer_of(0)).wait_recv()
    home(b_out.at[some], b_in.at[some], 1, peer_of(0)).wait_recv()
    home(c_out.at[some], c_in.at[some], 2, peer_of(0)).wait_recv()
    home(d_out.at[some], d_in.at[some], 3, peer_of(0)).wait_recv()

    for copy in keep:
        copy.wait()

    for part in range(2):
        to_peer(main_out.at[part, some], main_in.at[part, some], 2 * part, peer_of(0)).wait_send()
        to_peer(rest_out.at[part, some], rest_in.at[part, some], 2 * part + 1, peer_of(0)).wait_send()
    for kk in range(DIRS):

        @pl.when(borrower_ok[kk])
        def _():
            lend(kk).wait_send()

        @pl.when(lender_ok[kk])
        def _():
            give_back(kk).wait_send()

    home(a_out.at[some], a_in.at[some], 0, peer_of(0)).wait_send()
    home(b_out.at[some], b_in.at[some], 1, peer_of(0)).wait_send()
    home(c_out.at[some], c_in.at[some], 2, peer_of(0)).wait_send()
    home(d_out.at[some], d_in.at[some], 3, peer_of(0)).wait_send()


def per_device(heads, doms, queries, keys_in, values_in, grad_out, pos_bias, neighbours, send_block, orient):
    rows, width = queries.shape
    rest = rows - MAIN
    tokens = QB_DOM * BT
    whole = pl.BlockSpec(memory_space=pltpu.VMEM)
    anywhere = pl.BlockSpec(memory_space=pl.ANY)
    out = jax.ShapeDtypeStruct((rows, width), BF16)
    block = (BT, LANES)
    dma = pltpu.SemaphoreType.DMA
    arrivals = tuple(
        jax.ShapeDtypeStruct((heads, n, LANES), BF16) for n in (MAIN // 2, MAIN, rest, rest)
    )
    arrived = pl.pallas_call(
        functools.partial(kernel, heads, doms),
        out_shape=arrivals,
        in_specs=[anywhere] * 8,
        out_specs=(anywhere,) * 4,
        scratch_shapes=[
            *[pltpu.VMEM((rows, width), BF16)] * 4,
            pltpu.VMEM(pos_bias.shape, F32),
            pltpu.VMEM((2, heads, MAIN, LANES), BF16),
            pltpu.VMEM((2, heads, rest, LANES), BF16),
            pltpu.VMEM((2, heads, MAIN, LANES), BF16),
            pltpu.VMEM((2, heads, rest, LANES), BF16),
            pltpu.VMEM((tokens, LANES), F32),
            pltpu.VMEM((tokens, LANES), F32),
            pltpu.VMEM((SLOTS,) + block, BF16),
            pltpu.VMEM((DIRS, CAP) + block, BF16),
            pltpu.VMEM((DIRS, CAP) + block, BF16),
            pltpu.VMEM((DIRS, BT, BT), BF16),
            pltpu.VMEM((QB_DOM, WIN + 1) + block, F32),
            pltpu.VMEM((tokens, LANES), F32),
            pltpu.VMEM((tokens, LANES), F32),
            pltpu.VMEM((DIRS, CAP) + block, BF16),
            pltpu.VMEM((DIRS, CAP + 1) + block, BF16),
            pltpu.VMEM((heads, MAIN // 2, LANES), BF16),
            pltpu.VMEM((heads, MAIN, LANES), BF16),
            pltpu.VMEM((heads, rest, LANES), BF16),
            pltpu.VMEM((heads, rest, LANES), BF16),
            pltpu.SMEM((QB_DOM, WIN), jnp.int32),
            pltpu.SMEM((CAP, 1, DIRS), jnp.int32),
            pltpu.SMEM((1, DIRS), jnp.int32),
            pltpu.SMEM((QB_DOM, SLOTS), jnp.int32),
            pltpu.SMEM((QB_DOM, DIRS), jnp.int32),
            dma((8,)),
            dma((4,)),
            dma((4,)), dma((4, len(STAGES))),
            dma((DIRS,)), dma((DIRS,)),
            dma((DIRS,)), dma((DIRS,)),
            dma((4,)), dma((4,)),
        ],
        compiler_params=pltpu.CompilerParams(collective_id=0, has_side_effects=True),
    )(neighbours, jnp.transpose(send_block, (2, 0, 1)), orient, queries, keys_in, values_in, grad_out, pos_bias)
    return pl.pallas_call(
        lay_out, out_shape=(out, out, out), in_specs=[whole] * 4, out_specs=(whole, whole, whole),
    )(*arrived)


def solution(mesh):
    both = P(("dom", "head"), None)
    return jax.shard_map(
        functools.partial(per_device, mesh.shape["head"], mesh.shape["dom"]),
        mesh=mesh,
        in_specs=(both, both, both, both, P("head", None, None), P("dom", None), P("dom", None, None), P("dom", None)),
        out_specs=(both, both, both),
        check_vma=False,
    )
```

```python
import functools

import jax
import jax.numpy as jnp
from jax import lax
from jax.experimental import pallas as pl
from jax.experimental.pallas import tpu as pltpu
from jax.sharding import PartitionSpec as P

HD = 64
LANES = 128
PATCH = 8
BT = 64
GRID_ROWS = 4
DIRS = 8
WIN = 9
QB_DOM = 9
CAP = 3
MAIN = 16
SLOTS = QB_DOM + DIRS * CAP
OFFSETS = [(-1, -1), (-1, 0), (-1, 1), (0, -1), (0, 1), (1, -1), (1, 0), (1, 1)]
MESH = pl.DeviceIdType.MESH
STAGES = [(23, 31), (15, 23), (9, 15), (3, 9), (0, 3)]
STAGE_BLOCKS = [(0,), (1, 8), (2, 7), (3, 6), (4, 5)]
F32 = jnp.float32
BF16 = jnp.bfloat16


def live_slots(row_step, col_step):
    return 1 if row_step and col_step else CAP


def turn_matrix(orient_id):
    token = lax.broadcasted_iota(jnp.int32, (BT, BT), 0)
    target = lax.broadcasted_iota(jnp.int32, (BT, BT), 1)
    r = lax.shift_right_logical(token, 3)
    s = lax.bitwise_and(token, 7)
    flip_r = lax.bitwise_and(orient_id, 1)
    flip_s = lax.bitwise_and(lax.shift_right_logical(orient_id, 1), 1)
    swap = lax.bitwise_and(lax.shift_right_logical(orient_id, 2), 1)
    r2 = r + flip_r * (PATCH - 1 - 2 * r)
    s2 = s + flip_s * (PATCH - 1 - 2 * s)
    mapped = swap * (PATCH * s2 + r2) + (1 - swap) * (PATCH * r2 + s2)
    return jnp.where(target == mapped, 1.0, 0.0).astype(BF16)


def left_half(rows):
    return lax.broadcasted_iota(jnp.int32, (rows, LANES), 1) < HD


def swap_halves(x):
    return pltpu.roll(x, HD, 1)


def merge(x, y):
    mask = left_half(x.shape[0])
    return jnp.where(mask, x, swap_halves(y)), jnp.where(mask, swap_halves(x), y)


def lay_out(a_ref, b_ref, c_ref, d_ref, gq_ref, gk_ref, gv_ref):
    heads, half_main = a_ref.shape[:2]
    for i in range(heads // 2):
        cols = slice(i * LANES, (i + 1) * LANES)
        first, second = merge(a_ref[2 * i].astype(F32), a_ref[2 * i + 1].astype(F32))
        gq_ref[0:half_main, cols] = first.astype(BF16)
        gq_ref[half_main:MAIN, cols] = second.astype(BF16)
        first, second = merge(b_ref[2 * i].astype(F32), b_ref[2 * i + 1].astype(F32))
        gk_ref[0:MAIN, cols] = first.astype(BF16)
        gv_ref[0:MAIN, cols] = second.astype(BF16)
        first, second = merge(c_ref[2 * i].astype(F32), c_ref[2 * i + 1].astype(F32))
        gk_ref[MAIN:, cols] = first.astype(BF16)
        gv_ref[MAIN:, cols] = second.astype(BF16)
        first, _ = merge(d_ref[2 * i].astype(F32), d_ref[2 * i + 1].astype(F32))
        gq_ref[MAIN:, cols] = first.astype(BF16)


def kernel(
    heads, doms,
    near_any, send_any, orient_any, q_any, k_any, v_any, g_any, bias_any,
    a_in, b_in, c_in, d_in,
    q_ref, k_ref, v_ref, g_ref, bias_ref,
    main_out, rest_out, main_in, rest_in,
    pair_rows, qg_rows, ext, staged, arrived, turns,
    window_grads, gq_rows, total_rows, leaving, returned,
    a_out, b_out, c_out, d_out,
    near_ref, send_ref, orient_ref,
    inv_near, inv_send,
    load_sem, keep_sem,
    in_send, in_recv, dom_send, dom_recv, back_send, back_recv, out_send, out_recv,
):
    grid_cols = doms // GRID_ROWS
    peers = heads - 1
    me = lax.axis_index("head")
    dom = lax.axis_index("dom")
    row = dom // grid_cols
    col = dom % grid_cols
    scale = HD ** (-0.5)

    def inside(r, c):
        return (r >= 0) & (r < GRID_ROWS) & (c >= 0) & (c < grid_cols)

    lender_ok = [inside(row + dr, col + dc) for dr, dc in OFFSETS]
    borrower_ok = [inside(row - dr, col - dc) for dr, dc in OFFSETS]
    lender = [dom + dr * grid_cols + dc for dr, dc in OFFSETS]
    borrower = [dom - dr * grid_cols - dc for dr, dc in OFFSETS]

    def peer_of(n):
        half = (n + 1) // 2
        off = heads // 2 + half * (1 - 2 * (n % 2))
        return (me + off) % heads

    returned[:, CAP] = jnp.zeros((DIRS, BT, LANES), BF16)

    barrier = pltpu.get_barrier_semaphore()
    near_count = jnp.int32(peers)

    @pl.loop(0, peers)
    def _(n):
        pl.semaphore_signal(barrier, inc=1, device_id={"head": peer_of(n)}, device_id_type=MESH)

    for kk in range(DIRS):
        near_count = near_count + lender_ok[kk].astype(jnp.int32)

        @pl.when(lender_ok[kk])
        def _():
            pl.semaphore_signal(barrier, inc=1, device_id={"dom": lender[kk]}, device_id_type=MESH)

    pairs = ((k_any, k_ref), (v_any, v_ref), (q_any, q_ref), (g_any, g_ref), (bias_any, bias_ref),
             (near_any, near_ref), (send_any, send_ref), (orient_any, orient_ref))
    loads = [pltpu.make_async_copy(src, dst, load_sem.at[n]) for n, (src, dst) in enumerate(pairs)]
    for load in loads:
        load.start()

    def pack(part, first, second):
        for i in range(heads // 2):
            cols = slice(i * LANES, (i + 1) * LANES)
            x, y = first[0:MAIN, cols].astype(F32), second[0:MAIN, cols].astype(F32)
            even, odd = merge(x, y)
            main_out[part, 2 * i] = even.astype(BF16)
            main_out[part, 2 * i + 1] = odd.astype(BF16)
            x, y = first[MAIN:, cols].astype(F32), second[MAIN:, cols].astype(F32)
            even, odd = merge(x, y)
            rest_out[part, 2 * i] = even.astype(BF16)
            rest_out[part, 2 * i + 1] = odd.astype(BF16)
        main_in[part, me] = main_out[part, me]
        rest_in[part, me] = rest_out[part, me]

    def to_peer(src, dst, sem, peer, stage=0):
        return pltpu.make_async_remote_copy(
            src_ref=src, dst_ref=dst, send_sem=in_send.at[sem], recv_sem=in_recv.at[sem, stage],
            device_id={"head": peer}, device_id_type=MESH,
        )

    def send_rows(part, peer, stage=0):
        to_peer(main_out.at[part, peer], main_in.at[part, me], 2 * part, peer, stage).start()
        to_peer(rest_out.at[part, peer], rest_in.at[part, me], 2 * part + 1, peer, stage).start()

    loads[0].wait()
    loads[1].wait()
    pack(0, k_ref, v_ref)

    pl.semaphore_wait(barrier, near_count)

    @pl.loop(0, peers)
    def _(n):
        send_rows(0, peer_of(n))

    loads[2].wait()
    loads[3].wait()
    pack(1, q_ref, g_ref)

    for stage, (first, last) in reversed(list(enumerate(STAGES))):

        @pl.loop(first, last)
        def _(n):
            send_rows(1, peer_of(n), stage)

    window_grads[:, WIN] = jnp.zeros((QB_DOM, BT, LANES), F32)

    for load in loads[5:]:
        load.wait()

    def lent_block(kk, c):
        if live_slots(*OFFSETS[kk]) == CAP:
            return send_ref[c, 0, kk]
        return jnp.maximum(jnp.maximum(send_ref[0, 0, kk], send_ref[1, 0, kk]), send_ref[2, 0, kk])

    @pl.loop(0, QB_DOM)
    def _(b):
        names = [near_ref[b, j] for j in range(WIN)]

        def place(first, last):
            at = jnp.int32(WIN)
            for j in range(WIN):
                at = jnp.where((names[j] >= first) & (names[j] <= last), j, at)
            return at

        for e in range(QB_DOM):
            inv_near[b, e] = place(e, e)
        for kk, step in enumerate(OFFSETS):
            live = live_slots(*step)
            for c in range(live):
                e = QB_DOM + kk * CAP + c
                inv_near[b, e] = place(e, e + CAP - live)
        for kk, step in enumerate(OFFSETS):
            at = jnp.int32(CAP)
            for c in range(live_slots(*step)):
                at = jnp.where(borrower_ok[kk] & (lent_block(kk, c) == b), c, at)
            inv_send[b, kk] = at

    for kk in range(DIRS):
        turns[kk] = turn_matrix(orient_ref[0, kk])

    some = pl.ds(0, peers)

    def unpack_rows(part, rows):
        to_peer(main_out.at[part, some], main_in.at[part, some], 2 * part, peer_of(0)).wait_recv()
        to_peer(rest_out.at[part, some], rest_in.at[part, some], 2 * part + 1, peer_of(0)).wait_recv()
        count = MAIN + rest_in.shape[2]
        for source in range(heads):
            base = source * count
            rows[base:base + MAIN] = main_in[part, source].astype(F32)
            rows[base + MAIN:base + count] = rest_in[part, source].astype(F32)

    unpack_rows(0, pair_rows)
    for b in range(QB_DOM):
        ext[b] = pair_rows[b * BT:(b + 1) * BT].astype(BF16)

    def lend(kk):
        live = pl.ds(0, live_slots(*OFFSETS[kk]))
        return pltpu.make_async_remote_copy(
            src_ref=staged.at[kk, live], dst_ref=arrived.at[kk, live],
            send_sem=dom_send.at[kk], recv_sem=dom_recv.at[kk],
            device_id={"dom": borrower[kk]}, device_id_type=MESH,
        )

    for kk, step in enumerate(OFFSETS):
        for c in range(live_slots(*step)):
            staged[kk, c] = ext[lent_block(kk, c)]
    for kk in range(DIRS):

        @pl.when(borrower_ok[kk])
        def _():
            lend(kk).start()

    count = MAIN + rest_in.shape[2]

    def place_rows(source):
        base = source * count
        qg_rows[pl.ds(base, MAIN)] = main_in[1, source].astype(F32)
        qg_rows[pl.ds(base + MAIN, count - MAIN)] = rest_in[1, source].astype(F32)

    def stage_rows(stage):
        first, last = STAGES[stage]
        part = pl.ds(0, last - first)
        to_peer(main_out.at[1, part], main_in.at[1, part], 2, peer_of(0), stage).wait_recv()
        to_peer(rest_out.at[1, part], rest_in.at[1, part], 3, peer_of(0), stage).wait_recv()
        for n in range(first, last):
            place_rows(peer_of(n))

    place_rows(me)

    for kk, step in enumerate(OFFSETS):

        @pl.when(lender_ok[kk])
        def _():
            lend(kk).wait_recv()
            for c in range(live_slots(*step)):
                turned = jnp.dot(turns[kk], arrived[kk, c], preferred_element_type=F32).astype(BF16)
                for same in range(c, c + 1 + CAP - live_slots(*step)):
                    ext[QB_DOM + kk * CAP + same] = turned

    loads[4].wait()
    lane = lax.broadcasted_iota(jnp.int32, (1, LANES), 1)
    pair_scale = jnp.where(lane < HD, scale, 1.0).astype(F32)

    far_block = (me * count + count // 2) // BT

    def attend(b):
        rows = pl.ds(pl.multiple_of(b * BT, BT), BT)
        qg = qg_rows[rows]
        mask = left_half(BT)
        qg2 = jnp.concatenate([jnp.where(mask, qg, 0.0), jnp.where(mask, 0.0, qg)], axis=0).astype(BF16)
        window = jnp.concatenate([ext[near_ref[b, j]] for j in range(WIN)], axis=0)
        both = lax.dot_general(qg2, window, (((1,), (1,)), ((), ())), preferred_element_type=F32)
        scores = both[:BT] * scale + bias_ref[0]
        dprobs = both[BT:]
        top = jnp.max(scores, axis=1, keepdims=True)
        exps = jnp.exp(scores - top)
        probs = exps / jnp.sum(exps, axis=1, keepdims=True)
        half = probs.astype(BF16)
        delta = jnp.sum(half.astype(F32) * dprobs, axis=1, keepdims=True)
        dscores = (probs * (dprobs - delta)).astype(BF16)
        gq_rows[rows] = jnp.dot(dscores, window, preferred_element_type=F32) * scale
        stacked = jnp.concatenate([dscores, half], axis=0)
        grads = lax.dot_general(stacked, qg2, (((0,), (0,)), ((), ())), preferred_element_type=F32)
        grads = grads * pair_scale
        for j in range(WIN):
            window_grads[b, j] = grads[j * BT:(j + 1) * BT]

    for stage, blocks in enumerate(STAGE_BLOCKS):
        stage_rows(stage)
        for block in blocks:
            attend((far_block + block) % QB_DOM)

    def slot_grad(e):
        acc = window_grads[0, inv_near[0, e]]
        for b in range(1, QB_DOM):
            acc = acc + window_grads[b, inv_near[b, e]]
        return acc

    def give_back(kk):
        live = pl.ds(0, live_slots(*OFFSETS[kk]))
        return pltpu.make_async_remote_copy(
            src_ref=leaving.at[kk, live], dst_ref=returned.at[kk, live],
            send_sem=back_send.at[kk], recv_sem=back_recv.at[kk],
            device_id={"dom": lender[kk]}, device_id_type=MESH,
        )

    for kk, step in enumerate(OFFSETS):

        @pl.when(lender_ok[kk])
        def _():
            for c in range(live_slots(*step)):
                leaving[kk, c] = lax.dot_general(
                    turns[kk], slot_grad(QB_DOM + kk * CAP + c).astype(BF16),
                    (((0,), (0,)), ((), ())), preferred_element_type=F32,
                ).astype(BF16)

    for kk in range(DIRS):

        @pl.when(lender_ok[kk])
        def _():
            give_back(kk).start()

    def home(src, dst, sem, peer):
        return pltpu.make_async_remote_copy(
            src_ref=src, dst_ref=dst, send_sem=out_send.at[sem], recv_sem=out_recv.at[sem],
            device_id={"head": peer}, device_id_type=MESH,
        )

    half_main = MAIN // 2
    for peer in range(heads):
        base = peer * count
        first = gq_rows[base:base + half_main]
        second = gq_rows[base + half_main:base + MAIN]
        a_out[peer] = jnp.where(left_half(half_main), first, swap_halves(second)).astype(BF16)
        d_out[peer] = gq_rows[base + MAIN:base + count].astype(BF16)

    @pl.loop(0, peers)
    def _(n):
        peer = peer_of(n)
        home(a_out.at[peer], a_in.at[me], 0, peer).start()
        home(d_out.at[peer], d_in.at[me], 3, peer).start()

    keep = [
        pltpu.make_async_copy(src.at[me], dst.at[me], keep_sem.at[n])
        for n, (src, dst) in enumerate(((a_out, a_in), (b_out, b_in), (c_out, c_in), (d_out, d_in)))
    ]
    keep[0].start()
    keep[3].start()

    for b in range(QB_DOM):
        total_rows[b * BT:(b + 1) * BT] = slot_grad(b)

    for kk in range(DIRS):

        @pl.when(borrower_ok[kk])
        def _():
            give_back(kk).wait_recv()

    for b in range(QB_DOM):
        acc = total_rows[b * BT:(b + 1) * BT]
        for kk in range(DIRS):
            acc = acc + returned[kk, inv_send[b, kk]].astype(F32)
        total_rows[b * BT:(b + 1) * BT] = acc

    for peer in range(heads):
        base = peer * count
        b_out[peer] = total_rows[base:base + MAIN].astype(BF16)
        c_out[peer] = total_rows[base + MAIN:base + count].astype(BF16)

    @pl.loop(0, peers)
    def _(n):
        peer = peer_of(n)
        home(b_out.at[peer], b_in.at[me], 1, peer).start()
        home(c_out.at[peer], c_in.at[me], 2, peer).start()

    keep[1].start()
    keep[2].start()

    home(a_out.at[some], a_in.at[some], 0, peer_of(0)).wait_recv()
    home(b_out.at[some], b_in.at[some], 1, peer_of(0)).wait_recv()
    home(c_out.at[some], c_in.at[some], 2, peer_of(0)).wait_recv()
    home(d_out.at[some], d_in.at[some], 3, peer_of(0)).wait_recv()

    for copy in keep:
        copy.wait()

    for part in range(2):
        to_peer(main_out.at[part, some], main_in.at[part, some], 2 * part, peer_of(0)).wait_send()
        to_peer(rest_out.at[part, some], rest_in.at[part, some], 2 * part + 1, peer_of(0)).wait_send()
    for kk in range(DIRS):

        @pl.when(borrower_ok[kk])
        def _():
            lend(kk).wait_send()

        @pl.when(lender_ok[kk])
        def _():
            give_back(kk).wait_send()

    home(a_out.at[some], a_in.at[some], 0, peer_of(0)).wait_send()
    home(b_out.at[some], b_in.at[some], 1, peer_of(0)).wait_send()
    home(c_out.at[some], c_in.at[some], 2, peer_of(0)).wait_send()
    home(d_out.at[some], d_in.at[some], 3, peer_of(0)).wait_send()


def per_device(heads, doms, queries, keys_in, values_in, grad_out, pos_bias, neighbours, send_block, orient):
    rows, width = queries.shape
    rest = rows - MAIN
    tokens = QB_DOM * BT
    whole = pl.BlockSpec(memory_space=pltpu.VMEM)
    anywhere = pl.BlockSpec(memory_space=pl.ANY)
    out = jax.ShapeDtypeStruct((rows, width), BF16)
    block = (BT, LANES)
    dma = pltpu.SemaphoreType.DMA
    arrivals = tuple(
        jax.ShapeDtypeStruct((heads, n, LANES), BF16) for n in (MAIN // 2, MAIN, rest, rest)
    )
    arrived = pl.pallas_call(
        functools.partial(kernel, heads, doms),
        out_shape=arrivals,
        in_specs=[anywhere] * 8,
        out_specs=(anywhere,) * 4,
        scratch_shapes=[
            *[pltpu.VMEM((rows, width), BF16)] * 4,
            pltpu.VMEM(pos_bias.shape, F32),
            pltpu.VMEM((2, heads, MAIN, LANES), BF16),
            pltpu.VMEM((2, heads, rest, LANES), BF16),
            pltpu.VMEM((2, heads, MAIN, LANES), BF16),
            pltpu.VMEM((2, heads, rest, LANES), BF16),
            pltpu.VMEM((tokens, LANES), F32),
            pltpu.VMEM((tokens, LANES), F32),
            pltpu.VMEM((SLOTS,) + block, BF16),
            pltpu.VMEM((DIRS, CAP) + block, BF16),
            pltpu.VMEM((DIRS, CAP) + block, BF16),
            pltpu.VMEM((DIRS, BT, BT), BF16),
            pltpu.VMEM((QB_DOM, WIN + 1) + block, F32),
            pltpu.VMEM((tokens, LANES), F32),
            pltpu.VMEM((tokens, LANES), F32),
            pltpu.VMEM((DIRS, CAP) + block, BF16),
            pltpu.VMEM((DIRS, CAP + 1) + block, BF16),
            pltpu.VMEM((heads, MAIN // 2, LANES), BF16),
            pltpu.VMEM((heads, MAIN, LANES), BF16),
            pltpu.VMEM((heads, rest, LANES), BF16),
            pltpu.VMEM((heads, rest, LANES), BF16),
            pltpu.SMEM((QB_DOM, WIN), jnp.int32),
            pltpu.SMEM((CAP, 1, DIRS), jnp.int32),
            pltpu.SMEM((1, DIRS), jnp.int32),
            pltpu.SMEM((QB_DOM, SLOTS), jnp.int32),
            pltpu.SMEM((QB_DOM, DIRS), jnp.int32),
            dma((8,)),
            dma((4,)),
            dma((4,)), dma((4, len(STAGES))),
            dma((DIRS,)), dma((DIRS,)),
            dma((DIRS,)), dma((DIRS,)),
            dma((4,)), dma((4,)),
        ],
        compiler_params=pltpu.CompilerParams(collective_id=0, has_side_effects=True),
    )(neighbours, jnp.transpose(send_block, (2, 0, 1)), orient, queries, keys_in, values_in, grad_out, pos_bias)
    return pl.pallas_call(
        lay_out, out_shape=(out, out, out), in_specs=[whole] * 4, out_specs=(whole, whole, whole),
    )(*arrived)


def solution(mesh):
    both = P(("dom", "head"), None)
    return jax.shard_map(
        functools.partial(per_device, mesh.shape["head"], mesh.shape["dom"]),
        mesh=mesh,
        in_specs=(both, both, both, both, P("head", None, None), P("dom", None), P("dom", None, None), P("dom", None)),
        out_specs=(both, both, both),
        check_vma=False,
    )
```
